32 devices in a mesh: shard: 4 (over y, x), ctx: 8 (over z, core).
Axes of the slice: x: 2, y: 2, z: 4, core: 2. Of those that a mesh axis runs over, the one named last changes fastest.
Arguments:
- tokens: bfloat16 [16, 1024, 1152], P('shard', 'ctx'), may hold values from -6 to 6
- cotangent: bfloat16 [16, 1024, 1152], P('shard', 'ctx'), may hold values from -6 to 6
- pictures: int32 [16, 2], P('shard'), may hold values from 0 to 768, as said below
- w_query: bfloat16 [1152, 1024], P('shard'), may hold values from -0.1875 to 0.1875
- w_key: bfloat16 [1152, 256], P('shard'), may hold values from -0.1875 to 0.1875
- w_value: bfloat16 [1152, 256], P('shard'), may hold values from -0.1875 to 0.1875
- w_out: bfloat16 [1024, 1152], P('shard'), may hold values from -0.1875 to 0.1875
- w_gate: bfloat16 [1152, 6912], P('shard'), may hold values from -0.1875 to 0.1875
- w_up: bfloat16 [1152, 6912], P('shard'), may hold values from -0.1875 to 0.1875
- w_down: bfloat16 [6912, 1152], P('shard'), may hold values from -0.078125 to 0.078125
- g_attn_in: float32 [1152], P('shard'), may hold values from 0.5 to 1.5
- g_attn_out: float32 [1152], P('shard'), may hold values from 0.5 to 1.5
- g_ffn_in: float32 [1152], P('shard'), may hold values from 0.5 to 1.5
- g_ffn_out: float32 [1152], P('shard'), may hold values from 0.5 to 1.5
- g_query: float32 [256], P('shard'), may hold values from 0.5 to 1.5
- g_key: float32 [256], P('shard'), may hold values from 0.5 to 1.5
Outputs:
- output: bfloat16 [16, 1024, 1152], P('shard', 'ctx')
- input_grad: bfloat16 [16, 1024, 1152], P('shard', 'ctx')
- grad_w_query: float32 [1152, 1024], P('shard')
- grad_w_key: float32 [1152, 256], P('shard')
- grad_w_value: float32 [1152, 256], P('shard')
- grad_w_out: float32 [1024, 1152], P('shard')
- grad_w_gate: float32 [1152, 6912], P('shard')
- grad_w_up: float32 [1152, 6912], P('shard')
- grad_w_down: float32 [6912, 1152], P('shard')
- grad_g_attn_in: float32 [1152], P('shard')
- grad_g_attn_out: float32 [1152], P('shard')
- grad_g_ffn_in: float32 [1152], P('shard')
- grad_g_ffn_out: float32 [1152], P('shard')
- grad_g_query: float32 [256], P('shard')
- grad_g_key: float32 [256], P('shard')
The draws below stay inside these ranges and needn't reach their ends.
Inputs may be any that keep to these rules, and one draw needn't show every extreme that they name: `pictures`: piece j of a sequence lies wholly within the j-th of its 2 equal parts of 512 tokens, so pieces never meet.
All inputs are finite; a program needn't handle non-finite values.
Results may differ from the reference program's by a relative error of at most 0.04.
Values may be sent and summed in bfloat16 or wider, within the bound.
No kernel may reach another device: no remote copies, remote signals or barrier semaphores. Data moves between devices by JAX's collectives and lax.ppermute only.
A program may use at most 320 MiB of HBM per device.

```python
import jax
import jax.numpy as jnp
from jax import lax

D = 1152
HEADS = 4
HD = 256
FF = 6912
PICS = 2
PIECE = 256
LEN = 1024
SEQUENCES = 16


def draw_pictures(key, part):
    offsets = jax.random.randint(key, (SEQUENCES, PICS), 0, LEN // PICS - PIECE + 1).astype(jnp.int32)
    return offsets + (jnp.arange(PICS, dtype=jnp.int32) * (LEN // PICS))[None, :]


def block_levels(stream_key, shape, shards, least, largest):
    loudness, own = 1.0, jax.random.fold_in(stream_key, 6)
    for position, shards_of in shards:
        draws = jnp.exp(jax.random.uniform(jax.random.fold_in(own, position), (shards_of,), jnp.float32, least / len(shards), largest / len(shards)))
        loudness = loudness * jnp.repeat(draws, shape[position] // shards_of).reshape([-1 if axis == position else 1 for axis in range(len(shape))])
    return loudness


def bell_draw(stream_key, dims, width, most, split=(), kind=jnp.bfloat16):
    gain = block_levels(stream_key, dims, split, -0.22, 0.18) if split else 1.0
    drawn = jax.random.normal(stream_key, dims, jnp.float32) * width * gain
    return jnp.minimum(jnp.maximum(drawn, -most), most).astype(kind)


def setup_inputs(seed: int = 0) -> dict:
    splits = jax.random.split(jax.random.key(seed), 17)
    return {
        "tokens": bell_draw(splits[0], (SEQUENCES, LEN, D), 1.0, 6.0, ((0, 4), (1, 8))),
        "cotangent": bell_draw(splits[1], (SEQUENCES, LEN, D), 1.0, 6.0, ((0, 4), (1, 8))),
        "pictures": draw_pictures(jax.random.fold_in(splits[16], 71), 0),
        "w_query": bell_draw(splits[3], (D, HEADS * HD), D ** -0.5, 0.1875, ((0, 4),)),
        "w_key": bell_draw(splits[4], (D, HD), D ** -0.5, 0.1875, ((0, 4),)),
        "w_value": bell_draw(splits[5], (D, HD), D ** -0.5, 0.1875, ((0, 4),)),
        "w_out": bell_draw(splits[6], (HEADS * HD, D), (HEADS * HD) ** -0.5, 0.1875, ((0, 4),)),
        "w_gate": bell_draw(splits[7], (D, FF), D ** -0.5, 0.1875, ((0, 4),)),
        "w_up": bell_draw(splits[8], (D, FF), D ** -0.5, 0.1875, ((0, 4),)),
        "w_down": bell_draw(splits[9], (FF, D), FF ** -0.5, 0.078125, ((0, 4),)),
        "g_attn_in": jnp.clip(1.0 + 0.1 * jax.random.normal(splits[10], (D,), jnp.float32), 0.5, 1.5),
        "g_attn_out": jnp.clip(1.0 + 0.1 * jax.random.normal(splits[11], (D,), jnp.float32), 0.5, 1.5),
        "g_ffn_in": jnp.clip(1.0 + 0.1 * jax.random.normal(splits[12], (D,), jnp.float32), 0.5, 1.5),
        "g_ffn_out": jnp.clip(1.0 + 0.1 * jax.random.normal(splits[13], (D,), jnp.float32), 0.5, 1.5),
        "g_query": jnp.clip(1.0 + 0.1 * jax.random.normal(splits[14], (HD,), jnp.float32), 0.5, 1.5),
        "g_key": jnp.clip(1.0 + 0.1 * jax.random.normal(splits[15], (HD,), jnp.float32), 0.5, 1.5),
    }


@jax.custom_vjp
def low(v):
    return lax.optimization_barrier(v.astype(jnp.bfloat16)).astype(jnp.float32)

@jax.custom_vjp
def low_back(v):
    return v

def low_keep(v):
    return (low(v), None)

def low_pass(kept, grad):
    return (grad,)

def back_keep(v):
    return (v, None)

def back_low(kept, grad):
    return (low(grad),)
low.defvjp(low_keep, low_pass)
low_back.defvjp(back_keep, back_low)
epsilon = 1e-06
rope_base = 1000000.0
score_scale = 0.0625
highest = lax.Precision.HIGHEST

def normed(values_in, gain_vec):
    return values_in * lax.rsqrt(lax.optimization_barrier(jnp.mean(values_in * values_in, axis=-1, keepdims=True)) + epsilon) * gain_vec

def angles(positions, head_width):
    half_width = head_width // 2
    inverse = jnp.exp(-(jnp.arange(half_width).astype(jnp.float32) * 2.0 / head_width) * jnp.log(jnp.float32(rope_base)))
    return positions[:, None] * inverse[None, :]

def rotated(values_in, angle_table):
    half_width = values_in.shape[-1] // 2
    cosine = jnp.cos(angle_table)
    sine_part = jnp.sin(angle_table)
    front_half = values_in[..., :half_width]
    back_half = values_in[..., half_width:]
    return jnp.concatenate([front_half * cosine - back_half * sine_part, back_half * cosine + front_half * sine_part], axis=-1)

def allowed(query_pos, key_pos, starts):
    causal = key_pos[None, :] <= query_pos[:, None]
    inside_query = (query_pos[:, None] >= starts[None, :]) & (query_pos[:, None] < starts[None, :] + PIECE)
    inside_key = (key_pos[:, None] >= starts[None, :]) & (key_pos[:, None] < starts[None, :] + PIECE)
    shared = jnp.any(inside_query[:, None, :] & inside_key[None, :, :], axis=-1)
    return causal | shared

def geglu(gate_act, up_act):
    return jax.nn.gelu(gate_act, approximate=True) * up_act

def attend(queries, key_rows, value_rows, starts):
    length = queries.shape[0]
    block_rows = min(512, length)
    key_pos = jnp.arange(length, dtype=jnp.int32)

    def one_block(block_index):
        first_row = (block_index * block_rows).astype(jnp.int32)
        query_rows = lax.dynamic_slice_in_dim(queries, first_row, block_rows, 0)
        query_pos = first_row + jnp.arange(block_rows, dtype=jnp.int32)
        scores = jnp.einsum('qhd,kd->hqk', query_rows, key_rows, precision=highest) * score_scale
        scores = low_back(scores)
        scores = jnp.where(allowed(query_pos, key_pos, starts)[None], scores, -1e+30)
        peak_score = lax.optimization_barrier(jnp.max(scores, axis=-1, keepdims=True))
        exponent = jnp.exp(scores - peak_score)
        softmaxed = exponent / lax.optimization_barrier(jnp.sum(exponent, axis=-1, keepdims=True))
        return jnp.einsum('hqk,kd->qhd', low(softmaxed), value_rows, precision=highest)
    blocks = lax.map(jax.checkpoint(one_block), jnp.arange(length // block_rows, dtype=jnp.int32))
    return blocks.reshape(length, queries.shape[1], queries.shape[2])

def decoder_layer(seq_tokens, weights, starts):
    w_query, w_key, w_value, w_out, w_gate, w_up, w_down, g_attn_in, g_attn_out, g_ffn_in, g_ffn_out, g_query, g_key = weights
    length = seq_tokens.shape[0]
    angle_table = angles(jnp.arange(length).astype(jnp.float32), HD)
    normal_in = low(normed(seq_tokens, g_attn_in))
    query_raw = low_back(jnp.dot(normal_in, w_query, precision=highest))
    key_raw = low_back(jnp.dot(normal_in, w_key, precision=highest))
    value_rows = low(low_back(jnp.dot(normal_in, w_value, precision=highest)))
    queries = low(rotated(normed(query_raw.reshape(length, HEADS, HD), g_query), angle_table[:, None, :]))
    key_rows = low(rotated(normed(key_raw, g_key), angle_table))
    mixed = low(low_back(attend(queries, key_rows, value_rows, starts).reshape(length, HEADS * HD)))
    attn_out = low_back(jnp.dot(mixed, w_out, precision=highest))
    residual = seq_tokens + normed(attn_out, g_attn_out)
    normal_ffn = low(normed(residual, g_ffn_in))
    gate_act = low_back(jnp.dot(normal_ffn, w_gate, precision=highest))
    up_act = low_back(jnp.dot(normal_ffn, w_up, precision=highest))
    hidden = low(geglu(gate_act, up_act))
    branch = low_back(jnp.dot(hidden, w_down, precision=highest))
    return residual + normed(branch, g_ffn_out)

def reference(tokens, cotangent, pictures, w_query, w_key, w_value, w_out, w_gate, w_up, w_down, g_attn_in, g_attn_out, g_ffn_in, g_ffn_out, g_query, g_key):
    weights = tuple((w.astype(jnp.float32) for w in (w_query, w_key, w_value, w_out, w_gate, w_up, w_down, g_attn_in, g_attn_out, g_ffn_in, g_ffn_out, g_query, g_key)))

    def per_sequence(totals, sequence_item):
        seq_tokens, seq_grad, starts = sequence_item
        result, pullback = jax.vjp(lambda inputs, params: decoder_layer(inputs, params, starts), seq_tokens.astype(jnp.float32), weights)
        grad_in, grad_params = pullback(seq_grad.astype(jnp.float32))
        totals = tuple((t + g for t, g in zip(totals, grad_params)))
        return (totals, (result.astype(jnp.bfloat16), grad_in.astype(jnp.bfloat16)))
    starting = tuple((jnp.zeros(w.shape, jnp.float32) for w in weights))
    totals, (outputs, input_grads) = lax.scan(per_sequence, starting, (tokens, cotangent, pictures))
    return (outputs, input_grads, totals[0], totals[1], totals[2], totals[3], totals[4], totals[5], totals[6], totals[7], totals[8], totals[9], totals[10], totals[11], totals[12])
```

```python
import jax
import jax.numpy as jnp
from jax import lax
from jax.sharding import Mesh
from jax.sharding import PartitionSpec as P

HEADS = 4
HD = 256
PIECE = 256
EPS = 1e-06
ROPE_BASE = 1000000.0
SCALE = 0.0625
BF = jnp.bfloat16
F32 = jnp.float32


def dot(a, b):
    return lax.dot_general(a, b, (((1,), (0,)), ((), ())), preferred_element_type=F32)


def dot_t(a, b):
    return lax.dot_general(a, b, (((1,), (1,)), ((), ())), preferred_element_type=F32)


def dot_rows(a, b):
    return lax.dot_general(a, b, (((0,), (0,)), ((), ())), preferred_element_type=F32)


def inv_rms(v):
    return lax.rsqrt(jnp.mean(v * v, axis=-1, keepdims=True) + EPS)


def rms_back(v, r, gain, z):
    gz = gain * z
    return r * gz - v * (r * r * r * jnp.mean(gz * v, axis=-1, keepdims=True))


def rope(v, cos, sin):
    half = v.shape[-1] // 2
    a, b = v[..., :half], v[..., half:]
    return jnp.concatenate([a * cos - b * sin, b * cos + a * sin], axis=-1)


def gelu_and_slope(u):
    k = 0.7978845608028654
    u2 = u * u
    t = jnp.tanh(k * (u + 0.044715 * u2 * u))
    half = 0.5 * (1.0 + t)
    slope = half + 0.5 * u * (1.0 - t * t) * (k * (1.0 + 3.0 * 0.044715 * u2))
    return u * half, slope


def allowed(query_pos, key_pos, starts):
    causal = key_pos[None, :] <= query_pos[:, None]
    inside_query = (query_pos[:, None] >= starts[None, :]) & (
        query_pos[:, None] < starts[None, :] + PIECE
    )
    inside_key = (key_pos[:, None] >= starts[None, :]) & (
        key_pos[:, None] < starts[None, :] + PIECE
    )
    shared = jnp.any(inside_query[:, None, :] & inside_key[None, :, :], axis=-1)
    return causal | shared


def body(
    tokens,
    cotangent,
    pictures,
    w_query,
    w_key,
    w_value,
    w_out,
    w_gate,
    w_up,
    w_down,
    g_attn_in,
    g_attn_out,
    g_ffn_in,
    g_ffn_out,
    g_query,
    g_key,
):
    seqs, piece_len, width = tokens.shape
    n_s = lax.axis_size("shard")
    n_r = lax.axis_size("r")
    n_z = lax.axis_size("z")
    s, z, c = lax.axis_index("shard"), lax.axis_index("z"), lax.axis_index("c")
    own = seqs * piece_len
    both = 2 * own
    d_own = width // n_s
    ff = w_gate.shape[1]
    ff_own = ff // (2 * n_s)

    def px(v, k):
        return lax.ppermute(v, "shard", [(i, i ^ k) for i in range(n_s)])

    def pz(v, k):
        return lax.ppermute(v, "z", [(i, i ^ k) for i in range(n_z)])

    def pc(v):
        return lax.ppermute(v, "c", [(0, 1), (1, 0)])

    def natural(pieces, index):
        stacked = jnp.stack(pieces)
        n = len(pieces)
        return jnp.stack(
            [lax.dynamic_index_in_dim(stacked, index ^ j, 0, keepdims=False) for j in range(n)]
        )

    def pick(v, index, axis=0):
        return lax.dynamic_index_in_dim(v, index, axis, keepdims=False)

    def by_core(mine, other, axis):
        first = jnp.where(c == 0, mine, other)
        second = jnp.where(c == 0, other, mine)
        return jnp.stack([first, second], axis=axis)

    def gather4(v):
        h = v.shape[0] // 2
        f1, f2 = px(v, 1), px(v, 2)
        f3 = jnp.concatenate([px(f1[:h], 2), px(f2[h:], 1)])
        return [v, f1, f2, f3]

    def scatter4(p):
        h = p[0].shape[0] // 2
        a = px(p[3][:h].astype(BF), 2)
        b = px(p[3][h:].astype(BF), 1)
        q1 = jnp.concatenate([(p[1][:h] + a).astype(BF), p[1][h:].astype(BF)])
        q2 = jnp.concatenate([p[2][:h].astype(BF), (p[2][h:] + b).astype(BF)])
        return p[0] + px(q1, 1).astype(F32) + px(q2, 2).astype(F32)

    def sum_z(v):
        if n_z == 4:
            t = lax.ppermute(v, "z", [(0, 1), (3, 2)])
            part = v + t
            u = lax.ppermute(part, "z", [(1, 2), (2, 1)])
            total = part + u
            back = lax.ppermute(total, "z", [(1, 0), (2, 3)])
            v = jnp.where((z == 0) | (z == 3), back, total)
        else:
            v = lax.psum(v, "z")
        return lax.psum(v, "r") if n_r > 1 else v

    def to_sequence(v):
        got = [pick(v, z)] + [pz(pick(v, z ^ k), k) for k in range(1, n_z)]
        return natural(got, z)

    def from_sequence(v):
        got = [pick(v, z)] + [pz(pick(v, z ^ k), k) for k in range(1, n_z)]
        return natural(got, z)

    wq_half = lax.dynamic_slice_in_dim(w_query, c * (HEADS // 2 * HD), HEADS // 2 * HD, 1)
    wkv_half = jnp.where(c == 0, w_key, w_value)
    qkv_mine = jnp.concatenate([wq_half, wkv_half], axis=1)
    half_head = w_out.shape[0] // 2
    out_mine = lax.dynamic_slice_in_dim(w_out, c * half_head, half_head, 0)
    gains = jnp.concatenate([g_attn_in, g_attn_out, g_ffn_in, g_ffn_out, g_query, g_key])
    gains = natural([gains] + [px(gains, k) for k in range(1, n_s)], s)
    w_qkv = natural([qkv_mine] + [px(qkv_mine, k) for k in range(1, n_s)], s)
    w_qkv = w_qkv.reshape(width, qkv_mine.shape[1])
    w_qkv_other = pc(w_qkv)
    out_half = natural([out_mine] + [px(out_mine, k) for k in range(1, n_s)], s)
    w_out_all = by_core(out_half, pc(out_half), 1).reshape(HEADS * HD, width)
    x = to_sequence(tokens).reshape(own, width).astype(F32)
    zc = to_sequence(cotangent).reshape(own, width)

    def gain(first, size):
        return gains[:, first : first + size].reshape(1, n_s * size)

    hd_own = HD // n_s
    ga_in, ga_out, gf_in, gf_out = (gain(i * d_own, d_own) for i in range(4))
    gq, gk = gain(4 * d_own, hd_own), gain(4 * d_own + hd_own, hd_own)

    def col_piece(w, k):
        first = (s ^ k) * (2 * ff_own) + c * ff_own
        return lax.dynamic_slice_in_dim(w, first, ff_own, 1)

    gu = [jnp.stack([col_piece(w_gate, k), col_piece(w_up, k)]) for k in range(n_s)]
    gu = natural([gu[0]] + [px(gu[k], k) for k in range(1, n_s)], s)
    wg = gu[:, 0].reshape(width, ff_own)
    wu = gu[:, 1].reshape(width, ff_own)
    wd = lax.dynamic_slice_in_dim(w_down, c * ff_own, ff_own, 0)

    def whole(mine):
        n = mine.shape[1]
        mine = mine.reshape(seqs, piece_len, n)
        return by_core(mine, pc(mine), 1).reshape(both, n)

    def mine_of(v):
        n = v.shape[1]
        return pick(v.reshape(seqs, 2, piece_len, n), c, 1).reshape(own, n)

    r_x = inv_rms(x)
    nin = whole((x * r_x * ga_in).astype(BF))
    heads = HEADS // 2
    raw = dot(nin, w_qkv)
    raw_other = dot(nin, w_qkv_other[:, heads * HD :])
    q_raw = raw[:, : heads * HD].reshape(both, heads, HD)
    k_raw = jnp.where(c == 0, raw[:, heads * HD :], raw_other)
    v_raw = jnp.where(c == 0, raw_other, raw[:, heads * HD :])
    base = lax.axis_index("r") * both
    q_pos = base + jnp.arange(both, dtype=jnp.int32)
    half = HD // 2
    inverse = jnp.exp(
        -(jnp.arange(half).astype(F32) * 2.0 / HD) * jnp.log(jnp.float32(ROPE_BASE))
    )
    angle = q_pos.astype(F32)[:, None] * inverse[None, :]
    cos, sin = jnp.cos(angle), jnp.sin(angle)
    rq, rk = inv_rms(q_raw), inv_rms(k_raw)
    queries = rope(q_raw * rq * gq, cos[:, None, :], sin[:, None, :]).astype(BF)
    keys = rope(k_raw * rk * gk, cos, sin).astype(BF)
    values = v_raw.astype(BF)
    if n_r > 1:
        keys = lax.all_gather(keys, "r", axis=0, tiled=True)
        values = lax.all_gather(values, "r", axis=0, tiled=True)
    starts = pick(pictures, z)
    permitted = allowed(q_pos, jnp.arange(keys.shape[0], dtype=jnp.int32), starts)
    scores = jnp.einsum("qhd,kd->hqk", queries, keys, preferred_element_type=F32) * SCALE
    scores = jnp.where(permitted[None], scores, -1e30)
    peak = jnp.max(scores, axis=-1, keepdims=True)
    expo = jnp.exp(scores - peak)
    total = jnp.sum(expo, axis=-1, keepdims=True)
    soft = (expo / total).astype(BF)
    lse = peak + jnp.log(total)
    mixed = jnp.einsum("hqk,kd->qhd", soft, values, preferred_element_type=F32)
    mixed = mixed.astype(BF).reshape(both, heads * HD)
    mixed_other = pc(mixed)
    mixed_all = by_core(mixed, mixed_other, 1).reshape(both, HEADS * HD)
    attn_out = dot(mine_of(mixed_all), w_out_all)
    r_ao = inv_rms(attn_out)
    residual = x + attn_out * r_ao * ga_out
    r_res = inv_rms(residual)
    nffn = (residual * r_res * gf_in).astype(BF)

    rows = []
    acts = []
    branch_parts = []
    for v in gather4(nffn):
        rk_rows = jnp.concatenate([v, pc(v)])
        g_act, u_act = dot(rk_rows, wg), dot(rk_rows, wu)
        gel, _ = gelu_and_slope(g_act)
        hid = (gel * u_act).astype(BF)
        part = dot(hid, wd)
        branch_parts.append(part[:own] + pc(part[own:].astype(BF)))
        rows.append(rk_rows)
        acts.append((g_act, u_act, hid))
    branch = scatter4(branch_parts)
    r_b = inv_rms(branch)
    output = (residual + branch * r_b * gf_out).astype(BF)
    output = from_sequence(output.reshape(tokens.shape))

    zf = zc.astype(F32)
    gg_ffn_out = jnp.sum(zf * branch * r_b, axis=0)
    low = rms_back(branch, r_b, gf_out, zf).astype(BF)
    back_parts, gates, ups, lows = [], [], [], []
    for k, v in enumerate(gather4(low)):
        g_act, u_act, hid = acts[k]
        rk_low = jnp.concatenate([v, pc(v)])
        hid_grad = dot_t(rk_low, wd)
        gel, slope = gelu_and_slope(g_act)
        gate_grad = (hid_grad * u_act * slope).astype(BF)
        up_grad = (hid_grad * gel).astype(BF)
        part = dot_t(gate_grad, wg) + dot_t(up_grad, wu)
        back_parts.append(part[:own] + pc(part[own:].astype(BF)))
        gates.append(gate_grad)
        ups.append(up_grad)
        lows.append(rk_low)
    nffn_grad = scatter4(back_parts)
    all_rows = jnp.concatenate(rows)
    gw_down = dot_rows(jnp.concatenate([a[2] for a in acts]), jnp.concatenate(lows)).astype(BF)
    gw_gate = dot_rows(all_rows, jnp.concatenate(gates)).astype(BF)
    gw_up = dot_rows(all_rows, jnp.concatenate(ups)).astype(BF)

    hp = ff_own // 2
    gw_down = jnp.concatenate([sum_z(gw_down[:hp]), sum_z(gw_down[hp:])])
    gw_gu = jnp.stack([gw_gate.reshape(n_s, d_own, ff_own), gw_up.reshape(n_s, d_own, ff_own)], 1)
    gw_gu = [sum_z(pick(gw_gu, s))] + [sum_z(px(pick(gw_gu, s ^ k), k)) for k in range(1, n_s)]

    res_grad = zf + rms_back(residual, r_res, gf_in, nffn_grad)
    gg_ffn_in = jnp.sum(nffn_grad * residual * r_res, axis=0)
    gg_attn_out = jnp.sum(res_grad * attn_out * r_ao, axis=0)
    attn_grad = whole(rms_back(attn_out, r_ao, ga_out, res_grad).astype(BF))
    w_out_heads = lax.dynamic_slice_in_dim(w_out_all, c * heads * HD, heads * HD, 0)
    mixed_grad = dot_t(attn_grad, w_out_heads).astype(BF).reshape(both, heads, HD)
    scores = jnp.einsum("qhd,kd->hqk", queries, keys, preferred_element_type=F32) * SCALE
    scores = jnp.where(permitted[None], scores, -1e30)
    back = jnp.exp(scores - lse)
    prob_grad = jnp.einsum("qhd,kd->hqk", mixed_grad, values, preferred_element_type=F32)
    inner = jnp.sum(back * prob_grad, axis=-1, keepdims=True)
    score_grad = (back * (prob_grad - inner)).astype(BF)
    q_grad = jnp.einsum("hqk,kd->qhd", score_grad, keys, preferred_element_type=F32) * SCALE
    k_grad = jnp.einsum("hqk,qhd->kd", score_grad, queries, preferred_element_type=F32) * SCALE
    v_grad = jnp.einsum("hqk,qhd->kd", back.astype(BF), mixed_grad, preferred_element_type=F32)
    k_grad = k_grad + pc(k_grad.astype(BF)).astype(F32)
    v_grad = v_grad + pc(v_grad.astype(BF)).astype(F32)
    if n_r > 1:
        k_grad = lax.psum_scatter(k_grad.astype(BF), "r", scatter_dimension=0, tiled=True).astype(F32)
        v_grad = lax.psum_scatter(v_grad.astype(BF), "r", scatter_dimension=0, tiled=True).astype(F32)
    q_un = rope(q_grad, cos[:, None, :], -sin[:, None, :])
    k_un = rope(k_grad, cos, -sin)
    gg_query = jnp.sum(q_un * q_raw * rq, axis=(0, 1))
    gg_key = jnp.sum(mine_of(k_un * k_raw * rk), axis=0)
    q_low = rms_back(q_raw, rq, gq, q_un).astype(BF).reshape(both, heads * HD)
    k_low = rms_back(k_raw, rk, gk, k_un).astype(BF)
    v_low = v_grad.astype(BF)
    kv_mine = jnp.where(c == 0, k_low, v_low)
    kv_other = jnp.where(c == 0, v_low, k_low)
    low_mine = jnp.concatenate([q_low, kv_mine], axis=1)
    low_other = jnp.concatenate([pc(q_low), kv_other], axis=1)
    nin_grad = dot_t(mine_of(low_mine), w_qkv) + dot_t(mine_of(low_other), w_qkv_other)
    gg_attn_in = jnp.sum(nin_grad * x * r_x, axis=0)
    input_grad = (res_grad + rms_back(x, r_x, ga_in, nin_grad)).astype(BF)
    input_grad = from_sequence(input_grad.reshape(tokens.shape))

    gw_qkv = dot_rows(nin, low_mine)
    mixed_cols = mixed_all.reshape(both, HEADS, 2, HD // 2)
    mixed_cols = pick(mixed_cols, c, 2).reshape(both, HEADS * HD // 2)
    gw_out = dot_rows(mixed_cols, attn_grad)

    def to_shards(v):
        v = v.reshape(n_s, v.shape[0] // n_s, v.shape[1])
        return scatter4([pick(v, s ^ k) for k in range(n_s)]).astype(BF)

    gw_qkv = sum_z(to_shards(gw_qkv))
    gw_out = sum_z(to_shards(gw_out))

    parts = [gg_attn_in, gg_attn_out, gg_ffn_in, gg_ffn_out, gg_query, gg_key]
    small = jnp.concatenate([p.reshape(n_s, -1) for p in parts], axis=1)
    small = small + pc(small)
    for k in (1, 2) if n_z == 4 else ():
        small = small + pz(small, k)
    if n_z != 4:
        small = lax.psum(small, "z")
    if n_r > 1:
        small = lax.psum(small, "r")
    for k in (1, 2):
        small = small + px(small, k)
    small = pick(small, s)
    sizes = [d_own] * 4 + [hd_own] * 2
    small_out = []
    first = 0
    for size in sizes:
        small_out.append(small[first : first + size])
        first += size

    hw = heads * HD
    qkv_pair = by_core(gw_qkv, pc(gw_qkv), 0).astype(F32)
    gw_query = jnp.concatenate([qkv_pair[0][:, :hw], qkv_pair[1][:, :hw]], axis=1)
    gw_key, gw_value = qkv_pair[0][:, hw:], qkv_pair[1][:, hw:]
    gw_out = by_core(gw_out, pc(gw_out), 0).reshape(w_out.shape).astype(F32)
    gw_down = by_core(gw_down, pc(gw_down), 0).reshape(w_down.shape).astype(F32)
    pieces = natural([by_core(p, pc(p), 0) for p in gw_gu], s)
    gw_gate = jnp.concatenate(
        [pieces[j, i, 0] for j in range(n_s) for i in range(2)], axis=1
    ).astype(F32)
    gw_up = jnp.concatenate(
        [pieces[j, i, 1] for j in range(n_s) for i in range(2)], axis=1
    ).astype(F32)
    return (
        output,
        input_grad,
        gw_query,
        gw_key,
        gw_value,
        gw_out,
        gw_gate,
        gw_up,
        gw_down,
        *small_out,
    )


def solution(mesh):
    n_s, n_c = mesh.shape["shard"], mesh.shape["ctx"]

    def run(*args):
        seqs = args[0].shape[0] // n_s
        groups = n_c // (2 * seqs)
        fine = Mesh(mesh.devices.reshape(n_s, groups, seqs, 2), ("shard", "r", "z", "c"))
        ctx = ("r", "z", "c")
        rows, mat, vec = P("shard", ctx, None), P("shard", None), P("shard")
        return jax.shard_map(
            body,
            mesh=fine,
            in_specs=(rows, rows, mat) + (mat,) * 7 + (vec,) * 6,
            out_specs=(rows, rows) + (mat,) * 7 + (vec,) * 6,
            check_vma=False,
        )(*args)

    return run
```

```python
import functools

import jax
import jax.numpy as jnp
from jax import lax
from jax.experimental import pallas as pl
from jax.experimental.pallas import tpu as pltpu
from jax.sharding import Mesh
from jax.sharding import PartitionSpec as P

HEADS = 4
HD = 256
PIECE = 256
EPS = 1e-06
ROPE_BASE = 1000000.0
SCALE = 0.0625
BF = jnp.bfloat16
F32 = jnp.float32
VMEM = 56 * 1024 * 1024


def dot(a, b):
    return lax.dot_general(a, b, (((1,), (0,)), ((), ())), preferred_element_type=F32)


def dot_t(a, b):
    return lax.dot_general(a, b, (((1,), (1,)), ((), ())), preferred_element_type=F32)


def dot_rows(a, b):
    return lax.dot_general(a, b, (((0,), (0,)), ((), ())), preferred_element_type=F32)


def inv_rms(v):
    return lax.rsqrt(jnp.mean(v * v, axis=-1, keepdims=True) + EPS)


def rms_back(v, r, gain, z):
    gz = gain * z
    return r * gz - v * (r * r * r * jnp.mean(gz * v, axis=-1, keepdims=True))


def rope(v, cos, sin):
    half = v.shape[-1] // 2
    a, b = v[..., :half], v[..., half:]
    return jnp.concatenate([a * cos - b * sin, b * cos + a * sin], axis=-1)


def gelu_and_slope(u):
    k = 0.7978845608028654
    u2 = u * u
    t = jnp.tanh(k * (u + 0.044715 * u2 * u))
    half = 0.5 * (1.0 + t)
    slope = half + 0.5 * u * (1.0 - t * t) * (k * (1.0 + 3.0 * 0.044715 * u2))
    return u * half, slope


def call(kernel, grid, in_specs, out_specs, out_shape, flops, nbytes, scalars=0, scratch=(), exps=0):
    return pl.pallas_call(
        kernel,
        grid_spec=pltpu.PrefetchScalarGridSpec(
            num_scalar_prefetch=scalars,
            grid=grid,
            in_specs=in_specs,
            out_specs=out_specs,
            scratch_shapes=list(scratch),
        ),
        out_shape=out_shape,
        compiler_params=pltpu.CompilerParams(
            dimension_semantics=("arbitrary",) * len(grid), vmem_limit_bytes=VMEM
        ),
        cost_estimate=pl.CostEstimate(flops=flops, bytes_accessed=nbytes, transcendentals=exps),
    )


def full(shape):
    return pl.BlockSpec(shape, lambda *_: (0,) * len(shape))


def qkv_kernel(at, own, oth, w, ga, gq, gk, cos, sin, nin_o, raw_o, q_o, k_o, v_o):
    first = at[1] == 0
    a, b = own[0], oth[0]
    x = jnp.concatenate([jnp.where(first, a, b), jnp.where(first, b, a)]).astype(F32)
    nin = (x * inv_rms(x) * ga[...]).astype(BF)
    nin_o[...] = nin
    raw = dot(nin, w[...])
    raw_o[...] = raw[:, : 3 * HD]
    c, s = cos[...], sin[...]
    for h in range(2):
        q = raw[:, h * HD : (h + 1) * HD]
        q_o[:, h * HD : (h + 1) * HD] = rope(q * inv_rms(q) * gq[...], c, s).astype(BF)
    k = raw[:, 2 * HD : 3 * HD]
    k_o[...] = rope(k * inv_rms(k) * gk[...], c, s).astype(BF)
    v_o[...] = raw[:, 3 * HD :].astype(BF)


def project(at, own, oth, w, ga, gq, gk, cos, sin):
    seqs, n, width = own.shape
    rows = 2 * n * seqs
    cols = w.shape[1]
    block = pl.BlockSpec((1, n, width), lambda i, at: (i ^ at[0], 0, 0))

    def row(c):
        return pl.BlockSpec((2 * n, c), lambda i, at: (i, 0))

    shapes = [(width, BF), (3 * HD, F32), (2 * HD, BF), (HD, BF), (HD, BF)]
    return call(
        qkv_kernel,
        (seqs,),
        [block, block, full(w.shape), full(ga.shape), full(gq.shape), full(gk.shape), row(HD // 2), row(HD // 2)],
        [row(c) for c, _ in shapes],
        [jax.ShapeDtypeStruct((rows, c), t) for c, t in shapes],
        2 * rows * width * cols,
        rows * width * 8 + width * cols * 2,
        scalars=1,
    )(at, own, oth, w, ga, gq, gk, cos, sin)


def allowed(at, i, tile, length, transposed):
    a, b = (1, 0) if transposed else (0, 1)
    shape_q = (1, tile) if transposed else (tile, 1)
    shape_k = (length, 1) if transposed else (1, length)
    q = at[2] + i * tile + lax.broadcasted_iota(jnp.int32, shape_q, a)
    k = lax.broadcasted_iota(jnp.int32, shape_k, b)
    ok = k <= q
    for j in range(2):
        s = at[3 + j]
        ok = ok | (((q >= s) & (q < s + PIECE)) & ((k >= s) & (k < s + PIECE)))
    return ok


def attend_kernel(tile, at, q, k, v, o):
    s = dot_t(q[...], k[...]) * SCALE
    s = jnp.where(allowed(at, pl.program_id(1), tile, k.shape[0], False), s, -1e30)
    e = jnp.exp(s - jnp.max(s, axis=-1, keepdims=True))
    p = (e * (1.0 / jnp.sum(e, axis=-1, keepdims=True))).astype(BF)
    o[...] = dot(p, v[...]).astype(BF)


def attend(at, q, k, v, tile=256):
    rows, length = q.shape[0], k.shape[0]
    heads = q.shape[1] // HD
    qs = pl.BlockSpec((tile, HD), lambda h, i, at: (i, h))
    return call(
        functools.partial(attend_kernel, tile),
        (heads, rows // tile),
        [qs, full(k.shape), full(v.shape)],
        qs,
        jax.ShapeDtypeStruct(q.shape, BF),
        4 * rows * heads * length * HD,
        rows * heads * HD * 4 + length * HD * 4,
        scalars=1,
        exps=rows * heads * length,
    )(at, q, k, v)


def attend_back_kernel(tile, at, q, k, v, do, qraw, gq, cos, sin, dq_o, dk_o, dv_o, gg_o):
    @pl.when((pl.program_id(0) == 0) & (pl.program_id(1) == 0))
    def _():
        dk_o[...] = jnp.zeros_like(dk_o)
        dv_o[...] = jnp.zeros_like(dv_o)
        gg_o[...] = jnp.zeros_like(gg_o)

    s = dot_t(k[...], q[...]) * SCALE
    s = jnp.where(allowed(at, pl.program_id(1), tile, k.shape[0], True), s, -1e30)
    e = jnp.exp(s - jnp.max(s, axis=0, keepdims=True))
    p = e * (1.0 / jnp.sum(e, axis=0, keepdims=True))
    dp = dot_t(v[...], do[...])
    ds = (p * (dp - jnp.sum(p * dp, axis=0, keepdims=True))).astype(BF)
    dv_o[...] += dot(p.astype(BF), do[...])
    dk_o[...] += dot(ds, q[...]) * SCALE
    dq = dot_rows(ds, k[...]) * SCALE
    un = rope(dq, cos[...], -sin[...])
    raw = qraw[...]
    r = inv_rms(raw)
    gg_o[...] += jnp.sum(un * raw * r, axis=0, keepdims=True)
    dq_o[...] = rms_back(raw, r, gq[...], un).astype(BF)


def attend_back(at, q, k, v, do, raw, gq, cos, sin, tile=256):
    rows, length = q.shape[0], k.shape[0]
    heads = q.shape[1] // HD
    qs = pl.BlockSpec((tile, HD), lambda h, i, at: (i, h))
    cs = pl.BlockSpec((tile, HD // 2), lambda h, i, at: (i, 0))
    return call(
        functools.partial(attend_back_kernel, tile),
        (heads, rows // tile),
        [qs, full(k.shape), full(v.shape), qs, qs, full(gq.shape), cs, cs],
        [qs, full(k.shape), full(v.shape), full(gq.shape)],
        [
            jax.ShapeDtypeStruct(q.shape, BF),
            jax.ShapeDtypeStruct(k.shape, F32),
            jax.ShapeDtypeStruct(v.shape, F32),
            jax.ShapeDtypeStruct(gq.shape, F32),
        ],
        10 * rows * heads * length * HD,
        rows * heads * HD * 12 + length * HD * 12,
        scalars=1,
        exps=rows * heads * length,
    )(at, q, k, v, do, raw, gq, cos, sin)


def ffn_kernel(at, x, w, wd, g_o, u_o, h_o, p_o, acc):
    h = pl.program_id(0)
    xv = x[...]
    n_d, _, d, f = w.shape[1:]
    g = dot(xv, w[0, :, 0].reshape(n_d * d, f))
    u = dot(xv, w[0, :, 1].reshape(n_d * d, f))
    g_o[0] = g.astype(BF)
    u_o[0] = u.astype(BF)
    hid = (gelu_and_slope(g)[0] * u).astype(BF)
    h_o[0] = hid
    part = dot(hid, wd[...])

    @pl.when(h == 0)
    def _():
        acc[...] = part

    @pl.when(h == 1)
    def _():
        p_o[...] = (acc[...] + part).astype(p_o.dtype)


def ffn(at, x, w, wd, kind):
    rows, width = x.shape
    f = w.shape[-1]
    act = pl.BlockSpec((1, rows, f), lambda h, at: (h, 0, 0))
    return call(
        ffn_kernel,
        (2,),
        [
            full(x.shape),
            pl.BlockSpec((1,) + w.shape[1:], lambda h, at: (h, 0, 0, 0, 0)),
            pl.BlockSpec((f, width), lambda h, at: (h ^ at[1], 0)),
        ],
        [act, act, act, full(x.shape)],
        [jax.ShapeDtypeStruct((2, rows, f), BF)] * 3 + [jax.ShapeDtypeStruct(x.shape, kind)],
        12 * rows * width * f,
        12 * width * f + 16 * rows * f + 6 * rows * width,
        scalars=1,
        scratch=[pltpu.VMEM(x.shape, F32)],
        exps=2 * rows * f,
    )(at, x, w, wd)


def ffn_back_kernel(at, z, w, wd, g, u, gg_o, ug_o, p_o, acc):
    h = pl.program_id(0)
    n_d, _, d, f = w.shape[1:]
    hg = dot_t(z[...], wd[...])
    gel, slope = gelu_and_slope(g[0].astype(F32))
    gg = (hg * u[0].astype(F32) * slope).astype(BF)
    ug = (hg * gel).astype(BF)
    gg_o[0] = gg
    ug_o[0] = ug
    part = dot_t(gg, w[0, :, 0].reshape(n_d * d, f)) + dot_t(ug, w[0, :, 1].reshape(n_d * d, f))

    @pl.when(h == 0)
    def _():
        acc[...] = part

    @pl.when(h == 1)
    def _():
        p_o[...] = (acc[...] + part).astype(p_o.dtype)


def ffn_back(at, z, w, wd, g, u, kind):
    rows, width = z.shape
    f = w.shape[-1]
    act = pl.BlockSpec((1, rows, f), lambda h, at: (h, 0, 0))
    return call(
        ffn_back_kernel,
        (2,),
        [
            full(z.shape),
            pl.BlockSpec((1,) + w.shape[1:], lambda h, at: (h, 0, 0, 0, 0)),
            pl.BlockSpec((f, width), lambda h, at: (h ^ at[1], 0)),
            act,
            act,
        ],
        [act, act, full(z.shape)],
        [jax.ShapeDtypeStruct((2, rows, f), BF)] * 2 + [jax.ShapeDtypeStruct(z.shape, kind)],
        12 * rows * width * f,
        12 * width * f + 16 * rows * f + 6 * rows * width,
        scalars=1,
        scratch=[pltpu.VMEM(z.shape, F32)],
        exps=2 * rows * f,
    )(at, z, w, wd, g, u)


def gate_up_grad_kernel(n, add, *refs):
    x, g, u = refs[:n], refs[n : 2 * n], refs[2 * n : 3 * n]
    o = refs[-1]
    for m, v in ((0, g), (1, u)):
        total = dot_rows(x[0][...], v[0][0])
        for k in range(1, n):
            total += dot_rows(x[k][...], v[k][0])
        if add:
            total += refs[3 * n][m].astype(F32)
        o[m] = total.astype(BF)


def gate_up_grad(h, xs, gs, us, more, tile=384):
    n = len(xs)
    rows, width = xs[0].shape
    f = gs[0].shape[-1]
    out = pl.BlockSpec((2, tile, f), lambda i: (0, i, 0))
    return call(
        functools.partial(gate_up_grad_kernel, n, more is not None),
        (width // tile,),
        [pl.BlockSpec((rows, tile), lambda i: (0, i))] * n
        + [pl.BlockSpec((1, rows, f), lambda i: (h, 0, 0))] * (2 * n)
        + ([out] if more is not None else []),
        out,
        jax.ShapeDtypeStruct((2, width, f), BF),
        4 * n * rows * width * f,
        n * rows * (width + 2 * f) * 2 + 4 * width * f,
    )(*xs, *gs, *us, *([more] if more is not None else []))


def down_grad_kernel(n, add, *refs):
    hid, z = refs[:n], refs[n : 2 * n]
    o = refs[-1]
    total = dot_rows(hid[0][0], z[0][...])
    for k in range(1, n):
        total += dot_rows(hid[k][0], z[k][...])
    if add:
        total += refs[2 * n][...].astype(F32)
    o[...] = total.astype(BF)


def down_grad(h, hids, zs, more, tile=384):
    n = len(zs)
    rows, width = zs[0].shape
    f = hids[0].shape[-1]
    out = pl.BlockSpec((f, tile), lambda i: (0, i))
    return call(
        functools.partial(down_grad_kernel, n, more is not None),
        (width // tile,),
        [pl.BlockSpec((1, rows, f), lambda i: (h, 0, 0))] * n
        + [pl.BlockSpec((rows, tile), lambda i: (0, i))] * n
        + ([out] if more is not None else []),
        out,
        jax.ShapeDtypeStruct((f, width), BF),
        2 * n * rows * width * f,
        n * rows * (width + f) * 2 + 2 * width * f,
    )(*hids, *zs, *([more] if more is not None else []))


def lay_kernel(n_s, at, mine, oth, g_o, u_o):
    f = mine.shape[-1]
    first = at[1] == 0
    for m, o in ((0, g_o), (1, u_o)):
        for j in range(n_s):
            a, b = mine[0, j, m].astype(F32), oth[0, j, m].astype(F32)
            o[:, 2 * j * f : (2 * j + 1) * f] = jnp.where(first, a, b)
            o[:, (2 * j + 1) * f : (2 * j + 2) * f] = jnp.where(first, b, a)


def lay(at, mine, oth):
    n_z, n_s, _, rows, f = mine.shape
    block = pl.BlockSpec((1,) + mine.shape[1:], lambda i, at: (i, 0, 0, 0, 0))
    out = pl.BlockSpec((rows, 2 * n_s * f), lambda i, at: (i, 0))
    return call(
        functools.partial(lay_kernel, n_s),
        (n_z,),
        [block, block],
        [out, out],
        [jax.ShapeDtypeStruct((n_z * rows, 2 * n_s * f), F32)] * 2,
        0,
        n_z * n_s * rows * f * 24,
        scalars=1,
    )(at, mine, oth)


def body(
    tokens,
    cotangent,
    pictures,
    w_query,
    w_key,
    w_value,
    w_out,
    w_gate,
    w_up,
    w_down,
    g_attn_in,
    g_attn_out,
    g_ffn_in,
    g_ffn_out,
    g_query,
    g_key,
):
    seqs, piece_len, width = tokens.shape
    n_s = lax.axis_size("shard")
    n_r = lax.axis_size("r")
    n_z = lax.axis_size("z")
    s, z, c = lax.axis_index("shard"), lax.axis_index("z"), lax.axis_index("c")
    own = seqs * piece_len
    both = 2 * own
    heads = HEADS // 2
    hw = heads * HD
    d_own = width // n_s
    ff = w_gate.shape[1]
    ff_own = ff // (2 * n_s)

    def px(v, k):
        return lax.ppermute(v, "shard", [(i, i ^ k) for i in range(n_s)])

    def pz(v, k):
        return lax.ppermute(v, "z", [(i, i ^ k) for i in range(n_z)])

    def pc(v):
        return lax.ppermute(v, "c", [(0, 1), (1, 0)])

    def natural(pieces, index):
        stacked = jnp.stack(pieces)
        n = len(pieces)
        return jnp.stack(
            [lax.dynamic_index_in_dim(stacked, index ^ j, 0, keepdims=False) for j in range(n)]
        )

    def pick(v, index, axis=0):
        return lax.dynamic_index_in_dim(v, index, axis, keepdims=False)

    def by_core(mine, other, axis):
        first = jnp.where(c == 0, mine, other)
        second = jnp.where(c == 0, other, mine)
        return jnp.stack([first, second], axis=axis)

    def gather4(v):
        h = v.shape[0] // 2
        f1, f2 = px(v, 1), px(v, 2)
        f3 = jnp.concatenate([px(f1[:h], 2), px(f2[h:], 1)])
        return [v, f1, f2, f3]

    def scatter4(p):
        h = p[0].shape[0] // 2
        a = px(p[3][:h], 2)
        b = px(p[3][h:], 1)
        q1 = jnp.concatenate([p[1][:h] + a, p[1][h:]])
        q2 = jnp.concatenate([p[2][:h], p[2][h:] + b])
        return p[0] + px(q1, 1).astype(F32) + px(q2, 2).astype(F32)

    def sum_z(v):
        if n_z == 4:
            t = lax.ppermute(v, "z", [(0, 1), (3, 2)])
            part = v + t
            u = lax.ppermute(part, "z", [(1, 2), (2, 1)])
            total = part + u
            back = lax.ppermute(total, "z", [(1, 0), (2, 3)])
            v = jnp.where((z == 0) | (z == 3), back, total)
        else:
            v = lax.psum(v, "z")
        return lax.psum(v, "r") if n_r > 1 else v

    def spread(v):
        return jnp.stack([pick(v, z)] + [pz(pick(v, z ^ k), k) for k in range(1, n_z)])

    def in_order(v):
        return jnp.stack([pick(v, z ^ j) for j in range(n_z)])

    wq_half = lax.dynamic_slice_in_dim(w_query, c * hw, hw, 1)
    qkv_mine = jnp.concatenate([wq_half, w_key, w_value], axis=1)
    w_qkv = lax.all_gather(qkv_mine, "shard", axis=0, tiled=True)
    w_out_all = lax.all_gather(w_out, "shard", axis=0, tiled=True)
    x_near = spread(tokens)
    x_near_other = pc(x_near)
    gains = jnp.concatenate([g_attn_in, g_attn_out, g_ffn_in, g_ffn_out, g_query, g_key])
    gains = natural([gains] + [px(gains, k) for k in range(1, n_s)], s)

    def gain(first, size):
        return gains[:, first : first + size].reshape(1, n_s * size)

    hd_own = HD // n_s
    ga_in, ga_out, gf_in, gf_out = (gain(i * d_own, d_own) for i in range(4))
    gq, gk = gain(4 * d_own, hd_own), gain(4 * d_own + hd_own, hd_own)

    def col_piece(w, k):
        first = (s ^ k) * (2 * ff_own) + c * ff_own
        return lax.dynamic_slice_in_dim(w, first, ff_own, 1)

    gu = [jnp.stack([col_piece(w_gate, k), col_piece(w_up, k)]) for k in range(n_s)]
    gu = natural([gu[0]] + [px(gu[k], k) for k in range(1, n_s)], s)
    gu = jnp.stack([gu, pc(gu)])
    wq_other = pc(w_qkv[:, :hw])

    base = lax.axis_index("r") * both
    q_pos = base + jnp.arange(both, dtype=jnp.int32)
    half = HD // 2
    inverse = jnp.exp(
        -(jnp.arange(half).astype(F32) * 2.0 / HD) * jnp.log(jnp.float32(ROPE_BASE))
    )
    angle = q_pos.astype(F32)[:, None] * inverse[None, :]
    cos, sin = jnp.cos(angle), jnp.sin(angle)
    starts = pick(pictures, z)
    at = jnp.concatenate([jnp.stack([z, c, base]).astype(jnp.int32), starts.astype(jnp.int32)])

    def rows_of(v, core):
        n = v.shape[1]
        return pick(v.reshape(seqs, 2, piece_len, n), core, 1).reshape(own, n)

    def whole(mine):
        n = mine.shape[1]
        mine = mine.reshape(seqs, piece_len, n)
        return by_core(mine, pc(mine), 1).reshape(both, n)

    nin, raw, queries, keys, values = project(at, x_near, x_near_other, w_qkv, ga_in, gq, gk, cos, sin)
    if n_r > 1:
        keys = lax.all_gather(keys, "r", axis=0, tiled=True)
        values = lax.all_gather(values, "r", axis=0, tiled=True)
    mixed = attend(at, queries, keys, values)
    w_out_mine = lax.dynamic_slice_in_dim(w_out_all, c * hw, hw, 0)
    w_out_other = lax.dynamic_slice_in_dim(w_out_all, (1 - c) * hw, hw, 0)
    mixed_there = pc(rows_of(mixed, 1 - c))
    x = in_order(x_near).reshape(own, width).astype(F32)
    attn_out = dot(rows_of(mixed, c), w_out_mine) + dot(mixed_there, w_out_other)
    r_x = inv_rms(x)
    r_ao = inv_rms(attn_out)
    residual = x + attn_out * r_ao * ga_out
    r_res = inv_rms(residual)
    nffn = (residual * r_res * gf_in).astype(BF)

    rows = gather4(nffn)
    acts = [ffn(at, v, gu, w_down, F32 if k == 0 else BF) for k, v in enumerate(rows)]
    branch = scatter4([a[3] for a in acts])
    r_b = inv_rms(branch)
    output = (residual + branch * r_b * gf_out).astype(BF)
    output = in_order(spread(output.reshape(tokens.shape)))

    zf = in_order(spread(cotangent)).reshape(own, width).astype(F32)
    gg_ffn_out = jnp.sum(zf * branch * r_b, axis=0)
    lows = gather4(rms_back(branch, r_b, gf_out, zf).astype(BF))
    backs = [
        ffn_back(at, v, gu, w_down, acts[k][0], acts[k][1], F32 if k == 0 else BF)
        for k, v in enumerate(lows)
    ]
    nffn_grad = scatter4([b[2] for b in backs])
    hids = [a[2] for a in acts]
    gates, ups = [b[0] for b in backs], [b[1] for b in backs]
    gw_down = down_grad(0, hids, lows, pc(down_grad(1, hids, lows, None)))
    gw_gu = gate_up_grad(0, rows, gates, ups, pc(gate_up_grad(1, rows, gates, ups, None)))

    gw_down = lax.psum_scatter(gw_down, "z", scatter_dimension=0, tiled=True)
    dz = d_own // n_z
    gw_gu = gw_gu.reshape(2, n_s, n_z, dz, ff_own).transpose(2, 1, 0, 3, 4)
    gw_gu = lax.psum_scatter(gw_gu.reshape(-1, ff_own), "z", scatter_dimension=0, tiled=True)
    gw_gu = gw_gu.reshape(n_s, 2, dz, ff_own)
    if n_r > 1:
        gw_down, gw_gu = lax.psum(gw_down, "r"), lax.psum(gw_gu, "r")
    gw_gu = natural([pick(gw_gu, s)] + [px(pick(gw_gu, s ^ k), k) for k in range(1, n_s)], s)
    gw_down = lax.all_gather(gw_down, "z", axis=0, tiled=True)
    gw_gu = lax.all_gather(gw_gu.reshape(-1, ff_own), "z", axis=0, tiled=True)
    gw_gu = gw_gu.reshape(n_z, n_s, 2, dz, ff_own)

    res_grad = zf + rms_back(residual, r_res, gf_in, nffn_grad)
    gg_ffn_in = jnp.sum(nffn_grad * residual * r_res, axis=0)
    gg_attn_out = jnp.sum(res_grad * attn_out * r_ao, axis=0)
    attn_grad = whole(rms_back(attn_out, r_ao, ga_out, res_grad).astype(BF))
    mixed_grad = dot_t(attn_grad, w_out_mine).astype(BF)
    q_low, k_grad, v_grad, gg_query = attend_back(
        at, queries, keys, values, mixed_grad, raw, gq, cos, sin
    )
    k_grad = k_grad + pc(k_grad.astype(BF)).astype(F32)
    v_grad = v_grad + pc(v_grad.astype(BF)).astype(F32)
    if n_r > 1:
        k_grad = lax.psum_scatter(k_grad.astype(BF), "r", scatter_dimension=0, tiled=True).astype(F32)
        v_grad = lax.psum_scatter(v_grad.astype(BF), "r", scatter_dimension=0, tiled=True).astype(F32)
    k_raw = raw[:, hw:]
    rk = inv_rms(k_raw)
    k_un = rope(k_grad, cos, -sin)
    gg_key = jnp.sum(rows_of(k_un * k_raw * rk, c), axis=0)
    k_low = rms_back(k_raw, rk, gk, k_un).astype(BF)
    v_low = v_grad.astype(BF)
    low_own = jnp.concatenate([rows_of(q_low, c), rows_of(k_low, c), rows_of(v_low, c)], axis=1)
    nin_grad = dot_t(low_own, w_qkv) + dot_t(pc(rows_of(q_low, 1 - c)), wq_other)
    gg_attn_in = jnp.sum(nin_grad * x * r_x, axis=0)
    input_grad = (res_grad + rms_back(x, r_x, ga_in, nin_grad)).astype(BF)
    input_grad = in_order(spread(input_grad.reshape(tokens.shape)))

    low_mine = jnp.concatenate([q_low, jnp.where(c == 0, k_low, v_low)], axis=1)
    gw_qkv = dot_rows(nin, low_mine).astype(BF)
    gw_out = dot_rows(mixed, attn_grad).astype(BF).reshape(heads, 2, HD // 2, width)
    there = pc(pick(gw_out, 1 - c, 1))
    gw_out = by_core(pick(gw_out, c, 1), there, 0)

    def to_shards(v):
        v = v.reshape(n_s, v.size // (n_s * v.shape[-1]), v.shape[-1])
        parts = [pick(v, s ^ k) for k in range(n_s)]
        return scatter4([parts[0].astype(F32)] + parts[1:]).astype(BF)

    gw_qkv = sum_z(to_shards(gw_qkv))
    gw_out = sum_z(to_shards(gw_out))

    parts = [gg_attn_in, gg_attn_out, gg_ffn_in, gg_ffn_out, gg_query, gg_key]
    small = jnp.concatenate([p.reshape(n_s, -1) for p in parts], axis=1)
    small = small + pc(small)
    if n_z == 4:
        for k in (1, 2):
            small = small + pz(small, k)
    else:
        small = lax.psum(small, "z")
    if n_r > 1:
        small = lax.psum(small, "r")
    for k in (1, 2):
        small = small + px(small, k)
    small = pick(small, s)
    small_out = []
    first = 0
    for size in [d_own] * 4 + [hd_own] * 2:
        small_out.append(small[first : first + size])
        first += size

    qkv_pair = by_core(gw_qkv, pc(gw_qkv), 0).astype(F32)
    gw_query = jnp.concatenate([qkv_pair[0][:, :hw], qkv_pair[1][:, :hw]], axis=1)
    gw_key, gw_value = qkv_pair[0][:, hw:], qkv_pair[1][:, hw:]
    gw_out = by_core(gw_out, pc(gw_out), 0).reshape(w_out.shape).astype(F32)
    gw_down = by_core(gw_down, pc(gw_down), 0).reshape(w_down.shape).astype(F32)
    gw_gate, gw_up = lay(at, gw_gu, pc(gw_gu))
    return (
        output,
        input_grad,
        gw_query,
        gw_key,
        gw_value,
        gw_out,
        gw_gate,
        gw_up,
        gw_down,
        *small_out,
    )


def solution(mesh):
    n_s, n_c = mesh.shape["shard"], mesh.shape["ctx"]

    def run(*args):
        seqs = args[0].shape[0] // n_s
        groups = n_c // (2 * seqs)
        fine = Mesh(mesh.devices.reshape(n_s, groups, seqs, 2), ("shard", "r", "z", "c"))
        ctx = ("r", "z", "c")
        rows, mat, vec = P("shard", ctx, None), P("shard", None), P("shard")
        return jax.shard_map(
            body,
            mesh=fine,
            in_specs=(rows, rows, mat) + (mat,) * 7 + (vec,) * 6,
            out_specs=(rows, rows) + (mat,) * 7 + (vec,) * 6,
            check_vma=False,
        )(*args)

    return run
```

```python
import functools

import jax
import jax.numpy as jnp
from jax import lax
from jax.experimental import pallas as pl
from jax.experimental.pallas import tpu as pltpu
from jax.sharding import Mesh
from jax.sharding import PartitionSpec as P

HEADS = 4
HD = 256
PIECE = 256
EPS = 1e-06
ROPE_BASE = 1000000.0
SCALE = 0.0625
BF = jnp.bfloat16
F32 = jnp.float32
LANES = 128
ORDER = (0, 1, 3, 2)


def dot(a, b):
    return lax.dot_general(a, b, (((1,), (0,)), ((), ())), preferred_element_type=F32)


def dot_t(a, b):
    return lax.dot_general(a, b, (((1,), (1,)), ((), ())), preferred_element_type=F32)


def dot_rows(a, b):
    return lax.dot_general(a, b, (((0,), (0,)), ((), ())), preferred_element_type=F32)


def inv_rms(v):
    return lax.rsqrt(jnp.mean(v * v, axis=-1, keepdims=True) + EPS)


def rms_back(v, r, gain, z):
    gz = gain * z
    return r * gz - v * (r * r * r * jnp.mean(gz * v, axis=-1, keepdims=True))


def rope(v, cos, sin):
    half = v.shape[-1] // 2
    a, b = v[..., :half], v[..., half:]
    return jnp.concatenate([a * cos - b * sin, b * cos + a * sin], axis=-1)


def gelu_and_slope(u):
    k = 0.7978845608028654
    u2 = u * u
    t = jnp.tanh(k * (u + 0.044715 * u2 * u))
    half = 0.5 * (1.0 + t)
    slope = half + 0.5 * u * (1.0 - t * t) * (k * (1.0 + 3.0 * 0.044715 * u2))
    return u * half, slope


def call(kernel, grid, in_specs, out_specs, out_shape, flops, nbytes, scalars=0, scratch=(), exps=0, vmem=56):
    return pl.pallas_call(
        kernel,
        grid_spec=pltpu.PrefetchScalarGridSpec(
            num_scalar_prefetch=scalars,
            grid=grid,
            in_specs=in_specs,
            out_specs=out_specs,
            scratch_shapes=list(scratch),
        ),
        out_shape=out_shape,
        compiler_params=pltpu.CompilerParams(
            dimension_semantics=("arbitrary",) * len(grid), vmem_limit_bytes=vmem * 1024 * 1024
        ),
        cost_estimate=pl.CostEstimate(flops=flops, bytes_accessed=nbytes, transcendentals=exps),
    )


def full(shape):
    return pl.BlockSpec(shape, lambda *_: (0,) * len(shape))


def qkv_kernel(at, own, oth, w, ga, gq, gk, cos, sin, nin_o, raw_o, q_o, k_o, v_o):
    first = at[1] == 0
    a, b = own[0], oth[0]
    x = jnp.concatenate([jnp.where(first, a, b), jnp.where(first, b, a)]).astype(F32)
    nin = (x * inv_rms(x) * ga[...]).astype(BF)
    nin_o[...] = nin
    raw = dot(nin, w[...])
    raw_o[...] = raw[:, : 3 * HD]
    c, s = cos[...], sin[...]
    for h in range(2):
        q = raw[:, h * HD : (h + 1) * HD]
        q_o[:, h * HD : (h + 1) * HD] = rope(q * inv_rms(q) * (gq[...] * SCALE), c, s).astype(BF)
    k = raw[:, 2 * HD : 3 * HD]
    k_o[...] = rope(k * inv_rms(k) * gk[...], c, s).astype(BF)
    v_o[...] = raw[:, 3 * HD :].astype(BF)


def project(at, own, oth, w, ga, gq, gk, cos, sin):
    seqs, n, width = own.shape
    rows = 2 * n * seqs
    cols = w.shape[1]
    block = pl.BlockSpec((1, n, width), lambda i, at: (i ^ at[0], 0, 0))

    def row(c):
        return pl.BlockSpec((2 * n, c), lambda i, at: (i, 0))

    shapes = [(width, BF), (3 * HD, F32), (2 * HD, BF), (HD, BF), (HD, BF)]
    return call(
        qkv_kernel,
        (seqs,),
        [block, block, pl.BlockSpec(memory_space=pltpu.VMEM), full(ga.shape), full(gq.shape), full(gk.shape), row(HD // 2), row(HD // 2)],
        [row(c) for c, _ in shapes],
        [jax.ShapeDtypeStruct((rows, c), t) for c, t in shapes],
        2 * rows * width * cols,
        rows * width * 8 + width * cols * 2,
        scalars=1,
    )(at, own, oth, w, ga, gq, gk, cos, sin)


def reach(at, q):
    last = q
    for j in range(2):
        s = at[3 + j]
        last = jnp.where((q >= s) & (q < s + PIECE), s + (PIECE - 1), last)
    return last


def key_parts(at, tile, length):
    first = at[2] + pl.program_id(1) * tile
    last = first + tile - 1
    for j in range(2):
        s = at[3 + j]
        meets = (s < first + tile) & (s + PIECE > first)
        last = jnp.maximum(last, jnp.where(meets, s + (PIECE - 1), 0))
    return last // (length // 4) + 1


def tile_places(at, tile, shape, axis):
    return at[2] + pl.program_id(1) * tile + lax.broadcasted_iota(jnp.int32, shape, axis)


def attend_kernel(tile, at, q, k, v, o):
    length = k.shape[0]
    parts = key_parts(at, tile, length)
    last = reach(at, tile_places(at, tile, (tile, 1), 0))
    for n in range(1, 5):

        @pl.when(parts == n)
        def _():
            m = n * (length // 4)
            s = dot_t(q[...], k[:m])
            s = jnp.where(lax.broadcasted_iota(jnp.int32, (tile, m), 1) <= last, s, -1e30)
            e = jnp.exp(s - jnp.max(s, axis=-1, keepdims=True))
            p = (e * (1.0 / jnp.sum(e, axis=-1, keepdims=True))).astype(BF)
            o[...] = dot(p, v[:m]).astype(BF)


def attend(at, q, k, v, tile=256):
    rows, length = q.shape[0], k.shape[0]
    heads = q.shape[1] // HD
    qs = pl.BlockSpec((tile, HD), lambda h, i, at: (i, h))
    return call(
        functools.partial(attend_kernel, tile),
        (heads, rows // tile),
        [qs, full(k.shape), full(v.shape)],
        qs,
        jax.ShapeDtypeStruct(q.shape, BF),
        4 * rows * heads * length * HD,
        rows * heads * HD * 4 + length * HD * 4,
        scalars=1,
        exps=rows * heads * length,
    )(at, q, k, v)


def attend_back_kernel(tile, at, q, k, v, do, qraw, gq, cos, sin, dq_o, dk_o, dv_o, gg_o, dq_t):
    length = k.shape[0]

    @pl.when((pl.program_id(0) == 0) & (pl.program_id(1) == 0))
    def _():
        dk_o[...] = jnp.zeros_like(dk_o)
        dv_o[...] = jnp.zeros_like(dv_o)
        gg_o[...] = jnp.zeros_like(gg_o)

    parts = key_parts(at, tile, length)
    last = reach(at, tile_places(at, tile, (1, tile), 1))
    for n in range(1, 5):

        @pl.when(parts == n)
        def _():
            m = n * (length // 4)
            s = dot_t(k[:m], q[...])
            s = jnp.where(lax.broadcasted_iota(jnp.int32, (m, tile), 0) <= last, s, -1e30)
            e = jnp.exp(s - jnp.max(s, axis=0, keepdims=True))
            p = e * (1.0 / jnp.sum(e, axis=0, keepdims=True))
            dp = dot_t(v[:m], do[...])
            ds = (p * (dp - jnp.sum(p * dp, axis=0, keepdims=True))).astype(BF)
            dv_o[:m] += dot(p.astype(BF), do[...])
            dk_o[:m] += dot(ds, q[...])
            dq_t[...] = dot_rows(ds, k[:m])

    un = rope(dq_t[...] * SCALE, cos[...], -sin[...])
    raw = qraw[...]
    r = inv_rms(raw)
    gg_o[...] += jnp.sum(un * raw * r, axis=0, keepdims=True)
    dq_o[...] = rms_back(raw, r, gq[...], un).astype(BF)


def attend_back(at, q, k, v, do, raw, gq, cos, sin, tile=256):
    rows, length = q.shape[0], k.shape[0]
    heads = q.shape[1] // HD
    qs = pl.BlockSpec((tile, HD), lambda h, i, at: (i, h))
    cs = pl.BlockSpec((tile, HD // 2), lambda h, i, at: (i, 0))
    return call(
        functools.partial(attend_back_kernel, tile),
        (heads, rows // tile),
        [qs, full(k.shape), full(v.shape), qs, qs, full(gq.shape), cs, cs],
        [qs, full(k.shape), full(v.shape), full(gq.shape)],
        [
            jax.ShapeDtypeStruct(q.shape, BF),
            jax.ShapeDtypeStruct(k.shape, F32),
            jax.ShapeDtypeStruct(v.shape, F32),
            jax.ShapeDtypeStruct(gq.shape, F32),
        ],
        10 * rows * heads * length * HD,
        rows * heads * HD * 12 + length * HD * 12,
        scalars=1,
        scratch=[pltpu.VMEM((tile, HD), F32)],
        exps=rows * heads * length,
    )(at, q, k, v, do, raw, gq, cos, sin)


def ffn_kernel(x, w, wd, gel_o, slope_o, h_o, p_o):
    xv = x[...]
    u = dot(xv, w[1])
    gel, slope = gelu_and_slope(dot(xv, w[0]))
    hid = (gel * u).astype(BF)
    gel_o[...] = gel.astype(BF)
    slope_o[...] = (slope * u).astype(BF)
    h_o[...] = hid
    p_o[...] = dot(hid, wd[...]).astype(p_o.dtype)


def ffn(x, w, wd, kind, tile=256):
    rows, width = x.shape
    f = w.shape[-1]
    keep = pl.BlockSpec(memory_space=pltpu.VMEM)
    act = pl.BlockSpec((tile, f), lambda i: (i, 0))
    row = pl.BlockSpec((tile, width), lambda i: (i, 0))
    return call(
        ffn_kernel,
        (rows // tile,),
        [row, keep, keep],
        [act, act, act, row],
        [jax.ShapeDtypeStruct((rows, f), BF)] * 3 + [jax.ShapeDtypeStruct(x.shape, kind)],
        6 * rows * width * f,
        6 * width * f + 6 * rows * f + 4 * rows * width,
        exps=rows * f,
        vmem=40,
    )(x, w, wd)


def ffn_back_kernel(z, w, wd, gel, slope, gu_o, p_o):
    hg = dot_t(z[...], wd[...])
    gg = (hg * slope[...].astype(F32)).astype(BF)
    ug = (hg * gel[...].astype(F32)).astype(BF)
    gu_o[0] = gg
    gu_o[1] = ug
    p_o[...] = (dot_t(gg, w[0]) + dot_t(ug, w[1])).astype(p_o.dtype)


def ffn_back(z, w, wd, gel, slope, kind, tile=256):
    rows, width = z.shape
    f = w.shape[-1]
    keep = pl.BlockSpec(memory_space=pltpu.VMEM)
    act = pl.BlockSpec((tile, f), lambda i: (i, 0))
    row = pl.BlockSpec((tile, width), lambda i: (i, 0))
    return call(
        ffn_back_kernel,
        (rows // tile,),
        [row, keep, keep, act, act],
        [pl.BlockSpec((2, tile, f), lambda i: (0, i, 0)), row],
        [jax.ShapeDtypeStruct((2, rows, f), BF), jax.ShapeDtypeStruct(z.shape, kind)],
        6 * rows * width * f,
        6 * width * f + 6 * rows * f + 4 * rows * width,
        vmem=40,
    )(z, w, wd, gel, slope)


def columns_grad_kernel(n, *refs):
    x, g = refs[:n], refs[n : 2 * n]
    outs = refs[2 * n : 2 * n + 2]
    f = outs[0].shape[-1]
    xt = [x[k][...].T for k in range(n)]
    for i, o in enumerate(outs):
        total = dot(xt[0], g[0][0, :, i * f : (i + 1) * f])
        for k in range(1, n):
            total += dot(xt[k], g[k][0, :, i * f : (i + 1) * f])
        n_z, n_s, d, _ = o.shape
        for j in range(n_s):
            for q in range(n_z):
                first = (j * n_z + q) * d
                o[q, j] = total[first : first + d].astype(BF)


def columns_grad(m, xs, gus, form):
    n = len(xs)
    rows, width = xs[0].shape
    f = gus[0].shape[-1]
    out = full(form)
    return call(
        functools.partial(columns_grad_kernel, n),
        (1,),
        [full((rows, width))] * n + [pl.BlockSpec((1, rows, f), lambda i: (m, 0, 0))] * n,
        [out, out],
        [jax.ShapeDtypeStruct(form, BF)] * 2,
        2 * n * rows * width * f,
        n * rows * (width + f) * 2 + 2 * width * f,
    )(*xs, *gus)


def down_grad_kernel(n, *refs):
    hid, z = refs[:n], refs[n : 2 * n]
    outs = refs[2 * n :]
    f = hid[0].shape[-1] // 2
    for i, o in enumerate(outs):
        total = dot_rows(hid[0][:, i * f : (i + 1) * f], z[0][...])
        for k in range(1, n):
            total += dot_rows(hid[k][:, i * f : (i + 1) * f], z[k][...])
        o[...] = total[: o.shape[0]].astype(BF)


def down_grad(hids, zs, f_own):
    n = len(zs)
    rows, width = zs[0].shape
    f = hids[0].shape[-1]
    out = full((f_own, width))
    return call(
        functools.partial(down_grad_kernel, n),
        (1,),
        [full((rows, f))] * n + [full((rows, width))] * n,
        [out, out],
        [jax.ShapeDtypeStruct((f_own, width), BF)] * 2,
        2 * n * rows * width * f,
        n * rows * (width + f) * 2 + 2 * width * f,
    )(*hids, *zs)


def collect_kernel(n, at, *refs):
    o = refs[-1]
    d, f = refs[0].shape[1:]
    for h in range(2):
        for k in range(n):
            first = pl.multiple_of((at[5] ^ k) * d, d)
            for m in range(2):
                o[m, pl.ds(first, d), h * f : (h + 1) * f] = refs[h * n + k][m]


def collect(at, mine, other):
    n = len(mine)
    _, d, f = mine[0].shape
    keep = pl.BlockSpec(memory_space=pltpu.VMEM)
    shape = (2, n * d, 2 * f)
    return call(
        functools.partial(collect_kernel, n),
        (1,),
        [keep] * (2 * n),
        full(shape),
        jax.ShapeDtypeStruct(shape, BF),
        0,
        4 * n * d * f * 4,
        scalars=1,
        vmem=24,
    )(at, *mine, *other)


def fill_kernel(at, w, o):
    rows = w.shape[0]
    o[:rows] = w[...]
    o[rows:] = jnp.zeros((o.shape[0] - rows, o.shape[1]), BF)


def fill(at, w, f, pad):
    width = w.shape[1]
    return call(
        fill_kernel,
        (2,),
        [pl.BlockSpec((f, width), lambda h, at: (h ^ at[1], 0))],
        pl.BlockSpec((pad, width), lambda h, at: (h, 0)),
        jax.ShapeDtypeStruct((2 * pad, width), BF),
        0,
        8 * f * width,
        scalars=1,
    )(at, w)


def lay_kernel(f, at, mine, oth, g_o, u_o):
    first = at[1] == 0
    for j in range(mine.shape[1]):
        for m, o in ((0, g_o), (1, u_o)):
            a, b = mine[0, j, m, :, :f].astype(F32), oth[0, j, m, :, :f].astype(F32)
            o[:, 2 * j * f : (2 * j + 1) * f] = jnp.where(first, a, b)
            o[:, (2 * j + 1) * f : (2 * j + 2) * f] = jnp.where(first, b, a)


def lay(at, mine, other, f):
    n_z, n_s, _, rows, _ = mine.shape
    block = pl.BlockSpec((1,) + mine.shape[1:], lambda i, at: (i, 0, 0, 0, 0))
    out = pl.BlockSpec((rows, 2 * n_s * f), lambda i, at: (i, 0))
    return call(
        functools.partial(lay_kernel, f),
        (n_z,),
        [block, block],
        [out, out],
        [jax.ShapeDtypeStruct((n_z * rows, 2 * n_s * f), F32)] * 2,
        0,
        n_z * n_s * rows * f * 24,
        scalars=1,
    )(at, mine, other)


def body(
    tokens,
    cotangent,
    pictures,
    w_query,
    w_key,
    w_value,
    w_out,
    w_gate,
    w_up,
    w_down,
    g_attn_in,
    g_attn_out,
    g_ffn_in,
    g_ffn_out,
    g_query,
    g_key,
):
    seqs, piece_len, width = tokens.shape
    n_s = lax.axis_size("shard")
    n_r = lax.axis_size("r")
    n_z = lax.axis_size("z")
    s, z, c = lax.axis_index("shard"), lax.axis_index("z"), lax.axis_index("c")
    own = seqs * piece_len
    both = 2 * own
    heads = HEADS // 2
    hw = heads * HD
    d_own = width // n_s
    ff = w_gate.shape[1]
    ff_own = ff // (2 * n_s)
    ff_pad = -(-ff_own // LANES) * LANES

    def after(v, *others):
        return lax.optimization_barrier((v,) + others)[0]

    def px(v, k):
        return lax.ppermute(v, "shard", [(i, i ^ k) for i in range(n_s)])

    def pz(v, k):
        return lax.ppermute(v, "z", [(i, i ^ k) for i in range(n_z)])

    def pc(v):
        return lax.ppermute(v, "c", [(0, 1), (1, 0)])

    def natural(pieces, index):
        stacked = jnp.stack(pieces)
        n = len(pieces)
        return jnp.stack(
            [lax.dynamic_index_in_dim(stacked, index ^ j, 0, keepdims=False) for j in range(n)]
        )

    def pick(v, index, axis=0):
        return lax.dynamic_index_in_dim(v, index, axis, keepdims=False)

    def by_core(mine, other, axis):
        first = jnp.where(c == 0, mine, other)
        second = jnp.where(c == 0, other, mine)
        return jnp.stack([first, second], axis=axis)

    def gather4(v):
        h = v.shape[0] // 2
        f1, f2 = px(v, 1), px(v, 2)
        f3 = jnp.concatenate([px(f1[:h], 2), px(f2[h:], 1)])
        return [v, f1, f2, f3]

    def scatter_first(p):
        h = p[0].shape[0] // 2
        return px(p[3][:h], 2), px(p[3][h:], 1)

    def scatter_second(p, a, b):
        h = p[0].shape[0] // 2
        q1 = jnp.concatenate([p[1][:h] + a, p[1][h:]])
        q2 = jnp.concatenate([p[2][:h], p[2][h:] + b])
        return q1, q2

    def scatter_last(p, sent):
        return p[0] + px(sent[0], 1).astype(F32) + px(sent[1], 2).astype(F32)

    def scatter4(p):
        return scatter_last(p, scatter_second(p, *scatter_first(p)))

    class Line:
        def __init__(self, v):
            self.part = v
            self.got = lax.ppermute(v, "z", [(0, 1), (3, 2)]) if n_z == 4 else v

        def middle(self, *others):
            if n_z == 4:
                self.part = self.part + after(self.got, *others)
                self.got = lax.ppermute(self.part, "z", [(1, 2), (2, 1)])

        def last(self, *others):
            if n_z == 4:
                self.part = self.part + after(self.got, *others)
                self.got = lax.ppermute(self.part, "z", [(1, 0), (2, 3)])

        @property
        def total(self):
            return self.part

        def done(self, *others):
            if n_z != 4:
                return lax.psum(self.part, ("r", "z"))
            v = jnp.where((z == 0) | (z == 3), after(self.got, *others), self.part)
            return lax.psum(v, "r") if n_r > 1 else v

    def spread(v):
        return jnp.stack([pick(v, z)] + [pz(pick(v, z ^ k), k) for k in range(1, n_z)])

    def in_order(v):
        return jnp.stack([pick(v, z ^ j) for j in range(n_z)])

    wq_half = lax.dynamic_slice_in_dim(w_query, c * hw, hw, 1)
    qkv_mine = jnp.concatenate([wq_half, w_key, w_value], axis=1)
    w_qkv = lax.all_gather(qkv_mine, "shard", axis=0, tiled=True)
    half_head = w_out.shape[0] // 2
    out_mine = lax.dynamic_slice_in_dim(w_out, c * half_head, half_head, 0)
    out_mine = after(out_mine, w_qkv)
    out_half = [out_mine] + [px(out_mine, k) for k in range(1, n_s)]
    near = [pz(pick(tokens, z ^ k), k) for k in range(1, n_z)]
    x_near = jnp.stack([pick(tokens, z)] + near)
    x_near_other = pc(x_near)
    gains = jnp.concatenate([g_attn_in, g_attn_out, g_ffn_in, g_ffn_out, g_query, g_key])
    base = lax.axis_index("r") * both
    w_gate, w_up, w_down_late, gains, base = lax.optimization_barrier(
        (w_gate, w_up, w_down, gains, base, near[0])
    )[:5]
    gains = natural([gains] + [px(gains, k) for k in range(1, n_s)], s)

    def gain(first, size):
        return gains[:, first : first + size].reshape(1, n_s * size)

    hd_own = HD // n_s
    ga_in, ga_out, gf_in, gf_out = (gain(i * d_own, d_own) for i in range(4))
    gq, gk = gain(4 * d_own, hd_own), gain(4 * d_own + hd_own, hd_own)

    def col_piece(w, k):
        first = (s ^ k) * (2 * ff_own) + c * ff_own
        piece = lax.dynamic_slice_in_dim(w, first, ff_own, 1)
        return jnp.pad(piece, ((0, 0), (0, ff_pad - ff_own)))

    gu = [jnp.stack([col_piece(w_gate, k), col_piece(w_up, k)]) for k in range(n_s)]
    gu = [gu[0]] + list(lax.optimization_barrier((*gu[1:], out_mine))[: n_s - 1])
    gu = [gu[0]] + [px(gu[k], k) for k in range(1, n_s)]
    cot_near = spread(after(cotangent, x_near))

    q_pos = base + jnp.arange(both, dtype=jnp.int32)
    half = HD // 2
    inverse = jnp.exp(
        -(jnp.arange(half).astype(F32) * 2.0 / HD) * jnp.log(jnp.float32(ROPE_BASE))
    )
    angle = q_pos.astype(F32)[:, None] * inverse[None, :]
    cos, sin = jnp.cos(angle), jnp.sin(angle)
    starts = pick(pictures, z)
    at = jnp.concatenate([jnp.stack([z, c, base]).astype(jnp.int32), starts.astype(jnp.int32), s[None]])
    wd = fill(at, w_down_late, ff_own, ff_pad)
    x_near_other = after(x_near_other, wd)

    def rows_of(v, core):
        n = v.shape[1]
        return pick(v.reshape(seqs, 2, piece_len, n), core, 1).reshape(own, n)

    def whole(mine):
        n = mine.shape[1]
        mine = mine.reshape(seqs, piece_len, n)
        return by_core(mine, pc(mine), 1).reshape(both, n)

    nin, raw, queries, keys, values = project(at, x_near, x_near_other, w_qkv, ga_in, gq, gk, cos, sin)
    if n_r > 1:
        keys = lax.all_gather(keys, "r", axis=0, tiled=True)
        values = lax.all_gather(values, "r", axis=0, tiled=True)
    mixed = attend(at, queries, keys, values)
    out_half = natural(out_half, s)
    w_out_all = by_core(out_half, pc(out_half), 1).reshape(HEADS * HD, width)
    wq_other = pc(w_qkv[:, :hw])
    w_out_mine = lax.dynamic_slice_in_dim(w_out_all, c * hw, hw, 0)
    w_out_other = lax.dynamic_slice_in_dim(w_out_all, (1 - c) * hw, hw, 0)
    mixed_there = pc(rows_of(mixed, 1 - c))
    x = in_order(x_near).reshape(own, width).astype(F32)
    attn_out = dot(rows_of(mixed, c), w_out_mine) + dot(mixed_there, w_out_other)
    r_x = inv_rms(x)
    r_ao = inv_rms(attn_out)
    residual = x + attn_out * r_ao * ga_out
    r_res = inv_rms(residual)
    nffn = (residual * r_res * gf_in).astype(BF)

    rows = gather4(nffn)
    gu = list(lax.optimization_barrier((*gu, mixed))[:-1])
    gu = collect(at, gu, [pc(g) for g in gu])
    acts = [None] * n_s
    before = None
    for k in ORDER:
        v = rows[k] if before is None else after(rows[k], before)
        acts[k] = ffn(v, gu, wd, F32 if k == 0 else BF)
        before = acts[k][3]
    branch = scatter4([a[3] for a in acts])
    r_b = inv_rms(branch)
    output = (residual + branch * r_b * gf_out).astype(BF)
    output = in_order(spread(output.reshape(tokens.shape)))

    zf = in_order(cot_near).reshape(own, width).astype(F32)
    gg_ffn_out = jnp.sum(zf * branch * r_b, axis=0)
    lows = gather4(rms_back(branch, r_b, gf_out, zf).astype(BF))
    backs = [None] * n_s
    before = None
    for k in ORDER:
        v = lows[k] if before is None else after(lows[k], before)
        if k == ORDER[1]:
            v = after(v, output)
        if k == ORDER[2]:
            down_mine, down_other = down_grad([after(a[2], before) for a in acts], lows, ff_own)
            gw_down = down_mine + pc(down_other)
            before = gw_down
            v = after(v, gw_down)
        backs[k] = ffn_back(v, gu, wd, acts[k][0], acts[k][1], F32 if k == 0 else BF)
        before = backs[k][1]
    hop_a, hop_b = scatter_first([b[1] for b in backs])
    sent = scatter_second([b[1] for b in backs], hop_a, hop_b)
    gw_down = lax.psum_scatter(gw_down, "z", scatter_dimension=0, tiled=True)
    gus = [after(b[0], *sent, gw_down) for b in backs]
    form = (n_z, n_s, d_own // n_z, ff_pad)
    up_mine, up_other = columns_grad(1, rows, gus, form)
    nffn_grad = scatter_last([after(backs[0][1], up_mine)], sent)
    gus = [after(g, up_mine, nffn_grad) for g in gus]
    gate_mine, gate_other = columns_grad(0, rows, gus, form)

    def scatter_z(v):
        v = lax.psum_scatter(v, "z", scatter_dimension=0, tiled=True)
        return lax.psum(v, "r") if n_r > 1 else v

    def pieces(v):
        v = v.reshape(2, n_s, -1, ff_pad)
        v = natural([pick(v, s, 1)] + [px(pick(v, s ^ k, 1), k) for k in range(1, n_s)], s)
        v = lax.all_gather(v.reshape(-1, ff_pad), "z", axis=0, tiled=True)
        return v.reshape(n_z, n_s, 2, -1, ff_pad)

    if n_r > 1:
        gw_down = lax.psum(gw_down, "r")
    gw_down = lax.all_gather(gw_down, "z", axis=0, tiled=True)
    gw_up = up_mine + pc(up_other)
    gw_gate = gate_mine + pc(gate_other)
    gw_gu = jnp.stack([gw_gate, gw_up], axis=1).reshape(-1, ff_pad)
    nffn_grad = after(nffn_grad, gw_gu)
    gw_gu = scatter_z(gw_gu)

    res_grad = zf + rms_back(residual, r_res, gf_in, nffn_grad)
    gg_ffn_in = jnp.sum(nffn_grad * residual * r_res, axis=0)
    gg_attn_out = jnp.sum(res_grad * attn_out * r_ao, axis=0)
    attn_grad = whole(rms_back(attn_out, r_ao, ga_out, res_grad).astype(BF))
    def to_shards(v):
        v = v.reshape(n_s, v.size // (n_s * v.shape[-1]), v.shape[-1])
        parts = [pick(v, s ^ k) for k in range(n_s)]
        return scatter4([parts[0].astype(F32)] + parts[1:]).astype(BF)

    gw_out = dot_rows(mixed, attn_grad).astype(BF).reshape(heads, 2, HD // 2, width)
    there = pc(pick(gw_out, 1 - c, 1))
    gw_out = to_shards(by_core(pick(gw_out, c, 1), there, 0))
    mixed_grad = dot_t(attn_grad, w_out_mine).astype(BF)
    q_low, k_grad, v_grad, gg_query = attend_back(
        at, queries, keys, values, mixed_grad, raw, gq, cos, sin
    )
    k_grad = k_grad + pc(k_grad.astype(BF)).astype(F32)
    v_grad = v_grad + pc(v_grad.astype(BF)).astype(F32)
    if n_r > 1:
        k_grad = lax.psum_scatter(k_grad.astype(BF), "r", scatter_dimension=0, tiled=True).astype(F32)
        v_grad = lax.psum_scatter(v_grad.astype(BF), "r", scatter_dimension=0, tiled=True).astype(F32)
    k_raw = raw[:, hw:]
    rk = inv_rms(k_raw)
    k_un = rope(k_grad, cos, -sin)
    gg_key = jnp.sum(rows_of(k_un * k_raw * rk, c), axis=0)
    k_low = rms_back(k_raw, rk, gk, k_un).astype(BF)
    v_low = v_grad.astype(BF)
    low_own = jnp.concatenate([rows_of(q_low, c), rows_of(k_low, c), rows_of(v_low, c)], axis=1)
    nin_grad = dot_t(low_own, w_qkv) + dot_t(pc(rows_of(q_low, 1 - c)), wq_other)
    gg_attn_in = jnp.sum(nin_grad * x * r_x, axis=0)
    input_grad = (res_grad + rms_back(x, r_x, ga_in, nin_grad)).astype(BF)

    low_mine = jnp.concatenate([q_low, jnp.where(c == 0, k_low, v_low)], axis=1)
    gw_qkv = dot_rows(nin, low_mine).astype(BF)
    cols = gw_qkv.shape[1]
    parts = [gg_attn_in, gg_attn_out, gg_ffn_in, gg_ffn_out, gg_query, gg_key]
    small = jnp.concatenate([p.reshape(n_s, -1) for p in parts], axis=1)
    count = small.shape[1]
    out_rows = gw_out.size // cols
    extra = -(-(d_own + out_rows + -(-count // cols)) // (16 * n_z)) * (16 * n_z) - d_own - out_rows
    small = jnp.pad(small, ((0, 0), (0, extra * cols - count))).reshape(n_s, extra, cols)
    gw_qkv = jnp.concatenate([gw_qkv.reshape(n_s, d_own, cols), small.astype(BF)], axis=1)
    parts = [pick(gw_qkv, s ^ k) for k in range(n_s)]
    parts[0] = parts[0].astype(F32)
    hop_a, hop_b = scatter_first(parts)
    sent = scatter_second(parts, hop_a, hop_b)
    gw_qkv = scatter_last(parts, sent).astype(BF)
    line = Line(jnp.concatenate([gw_qkv, gw_out.reshape(out_rows, cols)]))
    gw_gu = pieces(after(gw_gu, gw_qkv))
    line.middle(gw_qkv)
    line.last(gw_qkv)
    gw_attn = line.done(gw_qkv)
    input_grad = after(input_grad, gw_gu)
    input_grad = in_order(spread(input_grad.reshape(tokens.shape)))

    attn_there = pc(gw_attn)
    gw_qkv, qkv_there = gw_attn[: d_own + extra], attn_there[: d_own + extra]
    gw_out, out_there = (
        v[d_own + extra :].reshape(half_head, width) for v in (gw_attn, attn_there)
    )
    small = (gw_qkv[d_own:].astype(F32) + qkv_there[d_own:].astype(F32)).reshape(-1)
    small_out = []
    first = 0
    for size in [d_own] * 4 + [hd_own] * 2:
        small_out.append(small[first : first + size])
        first += size
    qkv_pair = by_core(gw_qkv[:d_own], qkv_there[:d_own], 0).astype(F32)
    gw_query = jnp.concatenate([qkv_pair[0][:, :hw], qkv_pair[1][:, :hw]], axis=1)
    gw_key, gw_value = qkv_pair[0][:, hw:], qkv_pair[1][:, hw:]
    gw_out = by_core(gw_out, out_there, 0).reshape(w_out.shape).astype(F32)
    gw_down = by_core(gw_down, pc(gw_down), 0).reshape(w_down.shape).astype(F32)
    gw_gate, gw_up = lay(at, gw_gu, pc(gw_gu), ff_own)
    return (
        output,
        input_grad,
        gw_query,
        gw_key,
        gw_value,
        gw_out,
        gw_gate,
        gw_up,
        gw_down,
        *small_out,
    )


def solution(mesh):
    n_s, n_c = mesh.shape["shard"], mesh.shape["ctx"]

    def run(*args):
        seqs = args[0].shape[0] // n_s
        groups = n_c // (2 * seqs)
        fine = Mesh(mesh.devices.reshape(n_s, groups, seqs, 2), ("shard", "r", "z", "c"))
        ctx = ("r", "z", "c")
        rows, mat, vec = P("shard", ctx, None), P("shard", None), P("shard")
        return jax.shard_map(
            body,
            mesh=fine,
            in_specs=(rows, rows, mat) + (mat,) * 7 + (vec,) * 6,
            out_specs=(rows, rows) + (mat,) * 7 + (vec,) * 6,
            check_vma=False,
        )(*args)

    return run
```

```python
import functools

import jax
import jax.numpy as jnp
from jax import lax
from jax.experimental import pallas as pl
from jax.experimental.pallas import tpu as pltpu
from jax.sharding import Mesh
from jax.sharding import PartitionSpec as P

HEADS = 4
HD = 256
PIECE = 256
EPS = 1e-06
ROPE_BASE = 1000000.0
SCALE = 0.0625
BF = jnp.bfloat16
F32 = jnp.float32
LANES = 128
ORDER = (0, 1, 3, 2)


def dot(a, b):
    return lax.dot_general(a, b, (((1,), (0,)), ((), ())), preferred_element_type=F32)


def dot_t(a, b):
    return lax.dot_general(a, b, (((1,), (1,)), ((), ())), preferred_element_type=F32)


def dot_rows(a, b):
    return lax.dot_general(a, b, (((0,), (0,)), ((), ())), preferred_element_type=F32)


def inv_rms(v):
    return lax.rsqrt(jnp.mean(v * v, axis=-1, keepdims=True) + EPS)


def rms_back(v, r, gain, z):
    gz = gain * z
    return r * gz - v * (r * r * r * jnp.mean(gz * v, axis=-1, keepdims=True))


def rope(v, cos, sin):
    half = v.shape[-1] // 2
    a, b = v[..., :half], v[..., half:]
    return jnp.concatenate([a * cos - b * sin, b * cos + a * sin], axis=-1)


def gelu_and_slope(u):
    k = 0.7978845608028654
    u2 = u * u
    t = jnp.tanh(k * (u + 0.044715 * u2 * u))
    half = 0.5 * (1.0 + t)
    slope = half + 0.5 * u * (1.0 - t * t) * (k * (1.0 + 3.0 * 0.044715 * u2))
    return u * half, slope


def call(kernel, grid, in_specs, out_specs, out_shape, flops, nbytes, scalars=0, scratch=(), exps=0, vmem=56):
    return pl.pallas_call(
        kernel,
        grid_spec=pltpu.PrefetchScalarGridSpec(
            num_scalar_prefetch=scalars,
            grid=grid,
            in_specs=in_specs,
            out_specs=out_specs,
            scratch_shapes=list(scratch),
        ),
        out_shape=out_shape,
        compiler_params=pltpu.CompilerParams(
            dimension_semantics=("arbitrary",) * len(grid), vmem_limit_bytes=vmem * 1024 * 1024
        ),
        cost_estimate=pl.CostEstimate(flops=flops, bytes_accessed=nbytes, transcendentals=exps),
    )


def full(shape):
    return pl.BlockSpec(shape, lambda *_: (0,) * len(shape))


def qkv_kernel(at, own, oth, w, ga, gq, gk, cos, sin, nin_o, raw_o, q_o, k_o, v_o):
    first = at[1] == 0
    a, b = own[0], oth[0]
    x = jnp.concatenate([jnp.where(first, a, b), jnp.where(first, b, a)]).astype(F32)
    nin = (x * inv_rms(x) * ga[...]).astype(BF)
    nin_o[...] = nin
    raw = dot(nin, w[...])
    raw_o[...] = raw[:, : 3 * HD]
    c, s = cos[...], sin[...]
    for h in range(2):
        q = raw[:, h * HD : (h + 1) * HD]
        q_o[:, h * HD : (h + 1) * HD] = rope(q * inv_rms(q) * (gq[...] * SCALE), c, s).astype(BF)
    k = raw[:, 2 * HD : 3 * HD]
    k_o[...] = rope(k * inv_rms(k) * gk[...], c, s).astype(BF)
    v_o[...] = raw[:, 3 * HD :].astype(BF)


def project(at, own, oth, w, ga, gq, gk, cos, sin):
    seqs, n, width = own.shape
    rows = 2 * n * seqs
    cols = w.shape[1]
    block = pl.BlockSpec((1, n, width), lambda i, at: (i ^ at[0], 0, 0))

    def row(c):
        return pl.BlockSpec((2 * n, c), lambda i, at: (i, 0))

    shapes = [(width, BF), (3 * HD, F32), (2 * HD, BF), (HD, BF), (HD, BF)]
    return call(
        qkv_kernel,
        (seqs,),
        [block, block, pl.BlockSpec(memory_space=pltpu.VMEM), full(ga.shape), full(gq.shape), full(gk.shape), row(HD // 2), row(HD // 2)],
        [row(c) for c, _ in shapes],
        [jax.ShapeDtypeStruct((rows, c), t) for c, t in shapes],
        2 * rows * width * cols,
        rows * width * 8 + width * cols * 2,
        scalars=1,
    )(at, own, oth, w, ga, gq, gk, cos, sin)


def reach(at, q):
    last = q
    for j in range(2):
        s = at[3 + j]
        last = jnp.where((q >= s) & (q < s + PIECE), s + (PIECE - 1), last)
    return last


def key_parts(at, tile, length):
    first = at[2] + pl.program_id(1) * tile
    last = first + tile - 1
    for j in range(2):
        s = at[3 + j]
        meets = (s < first + tile) & (s + PIECE > first)
        last = jnp.maximum(last, jnp.where(meets, s + (PIECE - 1), 0))
    return last // (length // 4) + 1


def tile_places(at, tile, shape, axis):
    return at[2] + pl.program_id(1) * tile + lax.broadcasted_iota(jnp.int32, shape, axis)


def attend_kernel(tile, at, q, k, v, o):
    length = k.shape[0]
    parts = key_parts(at, tile, length)
    last = reach(at, tile_places(at, tile, (tile, 1), 0))
    for n in range(1, 5):

        @pl.when(parts == n)
        def _():
            m = n * (length // 4)
            s = dot_t(q[...], k[:m])
            s = jnp.where(lax.broadcasted_iota(jnp.int32, (tile, m), 1) <= last, s, -1e30)
            e = jnp.exp(s - jnp.max(s, axis=-1, keepdims=True))
            p = (e * (1.0 / jnp.sum(e, axis=-1, keepdims=True))).astype(BF)
            o[...] = dot(p, v[:m]).astype(BF)


def attend(at, q, k, v, tile=256):
    rows, length = q.shape[0], k.shape[0]
    heads = q.shape[1] // HD
    qs = pl.BlockSpec((tile, HD), lambda h, i, at: (i, h))
    return call(
        functools.partial(attend_kernel, tile),
        (heads, rows // tile),
        [qs, full(k.shape), full(v.shape)],
        qs,
        jax.ShapeDtypeStruct(q.shape, BF),
        4 * rows * heads * length * HD,
        rows * heads * HD * 4 + length * HD * 4,
        scalars=1,
        exps=rows * heads * length,
    )(at, q, k, v)


def attend_back_kernel(tile, at, q, k, v, do, qraw, gq, cos, sin, dq_o, dk_o, dv_o, gg_o, dq_t):
    length = k.shape[0]

    @pl.when((pl.program_id(0) == 0) & (pl.program_id(1) == 0))
    def _():
        dk_o[...] = jnp.zeros_like(dk_o)
        dv_o[...] = jnp.zeros_like(dv_o)
        gg_o[...] = jnp.zeros_like(gg_o)

    parts = key_parts(at, tile, length)
    last = reach(at, tile_places(at, tile, (1, tile), 1))
    for n in range(1, 5):

        @pl.when(parts == n)
        def _():
            m = n * (length // 4)
            s = dot_t(k[:m], q[...])
            s = jnp.where(lax.broadcasted_iota(jnp.int32, (m, tile), 0) <= last, s, -1e30)
            e = jnp.exp(s - jnp.max(s, axis=0, keepdims=True))
            p = e * (1.0 / jnp.sum(e, axis=0, keepdims=True))
            dp = dot_t(v[:m], do[...])
            ds = (p * (dp - jnp.sum(p * dp, axis=0, keepdims=True))).astype(BF)
            dv_o[:m] += dot(p.astype(BF), do[...])
            dk_o[:m] += dot(ds, q[...])
            dq_t[...] = dot_rows(ds, k[:m])

    un = rope(dq_t[...] * SCALE, cos[...], -sin[...])
    raw = qraw[...]
    r = inv_rms(raw)
    gg_o[...] += jnp.sum(un * raw * r, axis=0, keepdims=True)
    dq_o[...] = rms_back(raw, r, gq[...], un).astype(BF)


def attend_back(at, q, k, v, do, raw, gq, cos, sin, tile=256):
    rows, length = q.shape[0], k.shape[0]
    heads = q.shape[1] // HD
    qs = pl.BlockSpec((tile, HD), lambda h, i, at: (i, h))
    cs = pl.BlockSpec((tile, HD // 2), lambda h, i, at: (i, 0))
    return call(
        functools.partial(attend_back_kernel, tile),
        (heads, rows // tile),
        [qs, full(k.shape), full(v.shape), qs, qs, full(gq.shape), cs, cs],
        [qs, full(k.shape), full(v.shape), full(gq.shape)],
        [
            jax.ShapeDtypeStruct(q.shape, BF),
            jax.ShapeDtypeStruct(k.shape, F32),
            jax.ShapeDtypeStruct(v.shape, F32),
            jax.ShapeDtypeStruct(gq.shape, F32),
        ],
        10 * rows * heads * length * HD,
        rows * heads * HD * 12 + length * HD * 12,
        scalars=1,
        scratch=[pltpu.VMEM((tile, HD), F32)],
        exps=rows * heads * length,
    )(at, q, k, v, do, raw, gq, cos, sin)


def ffn_kernel(x, w, wd, gel_o, slope_o, h_o, p_o):
    xv = x[...]
    u = dot(xv, w[1])
    gel, slope = gelu_and_slope(dot(xv, w[0]))
    hid = (gel * u).astype(BF)
    gel_o[...] = gel.astype(BF)
    slope_o[...] = (slope * u).astype(BF)
    h_o[...] = hid
    p_o[...] = dot(hid, wd[...]).astype(p_o.dtype)


def ffn(x, w, wd, kind, tile=256):
    rows, width = x.shape
    f = w.shape[-1]
    keep = pl.BlockSpec(memory_space=pltpu.VMEM)
    act = pl.BlockSpec((tile, f), lambda i: (i, 0))
    row = pl.BlockSpec((tile, width), lambda i: (i, 0))
    return call(
        ffn_kernel,
        (rows // tile,),
        [row, keep, keep],
        [act, act, act, row],
        [jax.ShapeDtypeStruct((rows, f), BF)] * 3 + [jax.ShapeDtypeStruct(x.shape, kind)],
        6 * rows * width * f,
        6 * width * f + 6 * rows * f + 4 * rows * width,
        exps=rows * f,
        vmem=40,
    )(x, w, wd)


def ffn_back_kernel(z, w, wd, gel, slope, gu_o, p_o):
    hg = dot_t(z[...], wd[...])
    gg = (hg * slope[...].astype(F32)).astype(BF)
    ug = (hg * gel[...].astype(F32)).astype(BF)
    gu_o[0] = gg
    gu_o[1] = ug
    p_o[...] = (dot_t(gg, w[0]) + dot_t(ug, w[1])).astype(p_o.dtype)


def ffn_back(z, w, wd, gel, slope, kind, tile=256):
    rows, width = z.shape
    f = w.shape[-1]
    keep = pl.BlockSpec(memory_space=pltpu.VMEM)
    act = pl.BlockSpec((tile, f), lambda i: (i, 0))
    row = pl.BlockSpec((tile, width), lambda i: (i, 0))
    return call(
        ffn_back_kernel,
        (rows // tile,),
        [row, keep, keep, act, act],
        [pl.BlockSpec((2, tile, f), lambda i: (0, i, 0)), row],
        [jax.ShapeDtypeStruct((2, rows, f), BF), jax.ShapeDtypeStruct(z.shape, kind)],
        6 * rows * width * f,
        6 * width * f + 6 * rows * f + 4 * rows * width,
        vmem=40,
    )(z, w, wd, gel, slope)


def columns_grad_kernel(n, *refs):
    x, g = refs[:n], refs[n : 2 * n]
    outs, xt = refs[2 * n : 2 * n + 2], refs[-1]
    rows = x[0].shape[0]

    @pl.when(pl.program_id(0) == 0)
    def _():
        for k in range(n):
            xt[:, k * rows : (k + 1) * rows] = x[k][...].T

    total = dot(xt[:, :rows], g[0][0])
    for k in range(1, n):
        total += dot(xt[:, k * rows : (k + 1) * rows], g[k][0])
    n_z, n_s, d, _ = outs[0].shape
    for i, o in enumerate(outs):

        @pl.when(pl.program_id(0) == i)
        def _():
            for j in range(n_s):
                for q in range(n_z):
                    first = (j * n_z + q) * d
                    o[q, j] = total[first : first + d].astype(BF)


def columns_grad(m, xs, gus, form):
    n = len(xs)
    rows, width = xs[0].shape
    f = gus[0].shape[-1]
    out = full(form)
    return call(
        functools.partial(columns_grad_kernel, n),
        (2,),
        [full((rows, width))] * n + [pl.BlockSpec((1, rows, f // 2), lambda i: (m, 0, i))] * n,
        [out, out],
        [jax.ShapeDtypeStruct(form, BF)] * 2,
        2 * n * rows * width * f,
        n * rows * (width + f) * 2 + 2 * width * f,
        scratch=[pltpu.VMEM((width, n * rows), BF)],
    )(*xs, *gus)


def down_grad_kernel(n, *refs):
    hid, z = refs[:n], refs[n : 2 * n]
    total = dot_rows(hid[0][...], z[0][...])
    for k in range(1, n):
        total += dot_rows(hid[k][...], z[k][...])
    for i, o in enumerate(refs[2 * n :]):

        @pl.when(pl.program_id(0) == i)
        def _():
            o[...] = total[: o.shape[0]].astype(BF)


def down_grad(hids, zs, f_own):
    n = len(zs)
    rows, width = zs[0].shape
    f = hids[0].shape[-1]
    out = full((f_own, width))
    return call(
        functools.partial(down_grad_kernel, n),
        (2,),
        [pl.BlockSpec((rows, f // 2), lambda i: (0, i))] * n + [full((rows, width))] * n,
        [out, out],
        [jax.ShapeDtypeStruct((f_own, width), BF)] * 2,
        2 * n * rows * width * f,
        n * rows * (width + f) * 2 + 2 * width * f,
    )(*hids, *zs)


def collect_kernel(n, at, *refs):
    o = refs[-1]
    d, f = refs[0].shape[1:]
    for h in range(2):
        for k in range(n):
            first = pl.multiple_of((at[5] ^ k) * d, d)
            for m in range(2):
                o[m, pl.ds(first, d), h * f : (h + 1) * f] = refs[h * n + k][m]


def collect(at, mine, other):
    n = len(mine)
    _, d, f = mine[0].shape
    keep = pl.BlockSpec(memory_space=pltpu.VMEM)
    shape = (2, n * d, 2 * f)
    return call(
        functools.partial(collect_kernel, n),
        (1,),
        [keep] * (2 * n),
        full(shape),
        jax.ShapeDtypeStruct(shape, BF),
        0,
        4 * n * d * f * 4,
        scalars=1,
        vmem=24,
    )(at, *mine, *other)


def fill_kernel(at, w, o):
    rows = w.shape[0]
    o[:rows] = w[...]
    o[rows:] = jnp.zeros((o.shape[0] - rows, o.shape[1]), BF)


def fill(at, w, f, pad):
    width = w.shape[1]
    return call(
        fill_kernel,
        (2,),
        [pl.BlockSpec((f, width), lambda h, at: (h ^ at[1], 0))],
        pl.BlockSpec((pad, width), lambda h, at: (h, 0)),
        jax.ShapeDtypeStruct((2 * pad, width), BF),
        0,
        8 * f * width,
        scalars=1,
    )(at, w)


def lay_kernel(f, at, mine, oth, g_o, u_o):
    first = at[1] == 0
    for j in range(mine.shape[1]):
        for m, o in ((0, g_o), (1, u_o)):
            a, b = mine[0, j, m, :, :f].astype(F32), oth[0, j, m, :, :f].astype(F32)
            o[:, 2 * j * f : (2 * j + 1) * f] = jnp.where(first, a, b)
            o[:, (2 * j + 1) * f : (2 * j + 2) * f] = jnp.where(first, b, a)


def lay(at, mine, other, f):
    n_z, n_s, _, rows, _ = mine.shape
    block = pl.BlockSpec((1,) + mine.shape[1:], lambda i, at: (i, 0, 0, 0, 0))
    out = pl.BlockSpec((rows, 2 * n_s * f), lambda i, at: (i, 0))
    return call(
        functools.partial(lay_kernel, f),
        (n_z,),
        [block, block],
        [out, out],
        [jax.ShapeDtypeStruct((n_z * rows, 2 * n_s * f), F32)] * 2,
        0,
        n_z * n_s * rows * f * 24,
        scalars=1,
    )(at, mine, other)


def body(
    tokens,
    cotangent,
    pictures,
    w_query,
    w_key,
    w_value,
    w_out,
    w_gate,
    w_up,
    w_down,
    g_attn_in,
    g_attn_out,
    g_ffn_in,
    g_ffn_out,
    g_query,
    g_key,
):
    seqs, piece_len, width = tokens.shape
    n_s = lax.axis_size("shard")
    n_r = lax.axis_size("r")
    n_z = lax.axis_size("z")
    s, z, c = lax.axis_index("shard"), lax.axis_index("z"), lax.axis_index("c")
    own = seqs * piece_len
    both = 2 * own
    heads = HEADS // 2
    hw = heads * HD
    d_own = width // n_s
    ff = w_gate.shape[1]
    ff_own = ff // (2 * n_s)
    ff_pad = -(-ff_own // LANES) * LANES

    def after(v, *others):
        return lax.optimization_barrier((v,) + others)[0]

    def px(v, k):
        return lax.ppermute(v, "shard", [(i, i ^ k) for i in range(n_s)])

    def pz(v, k):
        return lax.ppermute(v, "z", [(i, i ^ k) for i in range(n_z)])

    def pc(v):
        return lax.ppermute(v, "c", [(0, 1), (1, 0)])

    def natural(pieces, index):
        stacked = jnp.stack(pieces)
        n = len(pieces)
        return jnp.stack(
            [lax.dynamic_index_in_dim(stacked, index ^ j, 0, keepdims=False) for j in range(n)]
        )

    def pick(v, index, axis=0):
        return lax.dynamic_index_in_dim(v, index, axis, keepdims=False)

    def by_core(mine, other, axis):
        first = jnp.where(c == 0, mine, other)
        second = jnp.where(c == 0, other, mine)
        return jnp.stack([first, second], axis=axis)

    def gather4(v):
        h = v.shape[0] // 2
        f1, f2 = px(v, 1), px(v, 2)
        f3 = jnp.concatenate([px(f1[:h], 2), px(f2[h:], 1)])
        return [v, f1, f2, f3]

    def scatter_first(p):
        h = p[0].shape[0] // 2
        return px(p[3][:h], 2), px(p[3][h:], 1)

    def scatter_second(p, a, b):
        h = p[0].shape[0] // 2
        q1 = jnp.concatenate([p[1][:h] + a, p[1][h:]])
        q2 = jnp.concatenate([p[2][:h], p[2][h:] + b])
        return q1, q2

    def scatter_last(p, sent):
        return p[0] + px(sent[0], 1).astype(F32) + px(sent[1], 2).astype(F32)

    def scatter4(p):
        return scatter_last(p, scatter_second(p, *scatter_first(p)))

    class Line:
        def __init__(self, v):
            self.part = v
            self.got = lax.ppermute(v, "z", [(0, 1), (3, 2)]) if n_z == 4 else v

        def middle(self, *others):
            if n_z == 4:
                self.part = self.part + after(self.got, *others)
                self.got = lax.ppermute(self.part, "z", [(1, 2), (2, 1)])

        def last(self, *others):
            if n_z == 4:
                self.part = self.part + after(self.got, *others)
                self.got = lax.ppermute(self.part, "z", [(1, 0), (2, 3)])

        @property
        def total(self):
            return self.part

        def done(self, *others):
            if n_z != 4:
                return lax.psum(self.part, ("r", "z"))
            v = jnp.where((z == 0) | (z == 3), after(self.got, *others), self.part)
            return lax.psum(v, "r") if n_r > 1 else v

    def spread(v):
        return jnp.stack([pick(v, z)] + [pz(pick(v, z ^ k), k) for k in range(1, n_z)])

    def in_order(v):
        return jnp.stack([pick(v, z ^ j) for j in range(n_z)])

    wq_half = lax.dynamic_slice_in_dim(w_query, c * hw, hw, 1)
    qkv_mine = jnp.concatenate([wq_half, w_key, w_value], axis=1)
    w_qkv = lax.all_gather(qkv_mine, "shard", axis=0, tiled=True)
    half_head = w_out.shape[0] // 2
    out_mine = lax.dynamic_slice_in_dim(w_out, c * half_head, half_head, 0)
    out_mine = after(out_mine, w_qkv)
    out_half = [out_mine] + [px(out_mine, k) for k in range(1, n_s)]
    near = [pz(pick(tokens, z ^ k), k) for k in range(1, n_z)]
    x_near = jnp.stack([pick(tokens, z)] + near)
    x_near_other = pc(x_near)
    gains = jnp.concatenate([g_attn_in, g_attn_out, g_ffn_in, g_ffn_out, g_query, g_key])
    base = lax.axis_index("r") * both
    w_gate, w_up, w_down_late, gains, base = lax.optimization_barrier(
        (w_gate, w_up, w_down, gains, base, near[0])
    )[:5]
    gains = natural([gains] + [px(gains, k) for k in range(1, n_s)], s)

    def gain(first, size):
        return gains[:, first : first + size].reshape(1, n_s * size)

    hd_own = HD // n_s
    ga_in, ga_out, gf_in, gf_out = (gain(i * d_own, d_own) for i in range(4))
    gq, gk = gain(4 * d_own, hd_own), gain(4 * d_own + hd_own, hd_own)

    def col_piece(w, k):
        first = (s ^ k) * (2 * ff_own) + c * ff_own
        piece = lax.dynamic_slice_in_dim(w, first, ff_own, 1)
        return jnp.pad(piece, ((0, 0), (0, ff_pad - ff_own)))

    gu = [jnp.stack([col_piece(w_gate, k), col_piece(w_up, k)]) for k in range(n_s)]
    gu = [gu[0]] + list(lax.optimization_barrier((*gu[1:], out_mine))[: n_s - 1])
    gu = [gu[0]] + [px(gu[k], k) for k in range(1, n_s)]
    cot_near = spread(after(cotangent, x_near))

    q_pos = base + jnp.arange(both, dtype=jnp.int32)
    half = HD // 2
    inverse = jnp.exp(
        -(jnp.arange(half).astype(F32) * 2.0 / HD) * jnp.log(jnp.float32(ROPE_BASE))
    )
    angle = q_pos.astype(F32)[:, None] * inverse[None, :]
    cos, sin = jnp.cos(angle), jnp.sin(angle)
    starts = pick(pictures, z)
    at = jnp.concatenate([jnp.stack([z, c, base]).astype(jnp.int32), starts.astype(jnp.int32), s[None]])
    wd = fill(at, w_down_late, ff_own, ff_pad)
    x_near_other = after(x_near_other, wd)

    def rows_of(v, core):
        n = v.shape[1]
        return pick(v.reshape(seqs, 2, piece_len, n), core, 1).reshape(own, n)

    def whole(mine):
        n = mine.shape[1]
        mine = mine.reshape(seqs, piece_len, n)
        return by_core(mine, pc(mine), 1).reshape(both, n)

    nin, raw, queries, keys, values = project(at, x_near, x_near_other, w_qkv, ga_in, gq, gk, cos, sin)
    if n_r > 1:
        keys = lax.all_gather(keys, "r", axis=0, tiled=True)
        values = lax.all_gather(values, "r", axis=0, tiled=True)
    mixed = attend(at, queries, keys, values)
    out_half = natural(out_half, s)
    w_out_all = by_core(out_half, pc(out_half), 1).reshape(HEADS * HD, width)
    wq_other = pc(w_qkv[:, :hw])
    w_out_mine = lax.dynamic_slice_in_dim(w_out_all, c * hw, hw, 0)
    w_out_other = lax.dynamic_slice_in_dim(w_out_all, (1 - c) * hw, hw, 0)
    mixed_there = pc(rows_of(mixed, 1 - c))
    x = in_order(x_near).reshape(own, width).astype(F32)
    attn_out = dot(rows_of(mixed, c), w_out_mine) + dot(mixed_there, w_out_other)
    r_x = inv_rms(x)
    r_ao = inv_rms(attn_out)
    residual = x + attn_out * r_ao * ga_out
    r_res = inv_rms(residual)
    nffn = (residual * r_res * gf_in).astype(BF)

    rows = gather4(nffn)
    gu = list(lax.optimization_barrier((*gu, mixed))[:-1])
    gu = collect(at, gu, [pc(g) for g in gu])
    acts = [None] * n_s
    before = None
    for k in ORDER:
        v = rows[k] if before is None else after(rows[k], before)
        acts[k] = ffn(v, gu, wd, F32 if k == 0 else BF)
        before = acts[k][3]
    branch = scatter4([a[3] for a in acts])
    r_b = inv_rms(branch)
    output = (residual + branch * r_b * gf_out).astype(BF)
    output = in_order(spread(output.reshape(tokens.shape)))

    zf = in_order(cot_near).reshape(own, width).astype(F32)
    gg_ffn_out = jnp.sum(zf * branch * r_b, axis=0)
    lows = gather4(rms_back(branch, r_b, gf_out, zf).astype(BF))
    backs = [None] * n_s
    before = None
    for k in ORDER:
        v = lows[k] if before is None else after(lows[k], before)
        if k == ORDER[1]:
            v = after(v, output)
        if k == ORDER[2]:
            down_mine, down_other = down_grad([after(a[2], before) for a in acts], lows, ff_own)
            gw_down = down_mine + pc(down_other)
            before = gw_down
            v = after(v, gw_down)
        backs[k] = ffn_back(v, gu, wd, acts[k][0], acts[k][1], F32 if k == 0 else BF)
        before = backs[k][1]
    hop_a, hop_b = scatter_first([b[1] for b in backs])
    sent = scatter_second([b[1] for b in backs], hop_a, hop_b)
    gw_down = lax.psum_scatter(gw_down, "z", scatter_dimension=0, tiled=True)
    gus = [after(b[0], *sent, gw_down) for b in backs]
    form = (n_z, n_s, d_own // n_z, ff_pad)
    up_mine, up_other = columns_grad(1, rows, gus, form)
    nffn_grad = scatter_last([after(backs[0][1], up_mine)], sent)
    gus = [after(g, up_mine, nffn_grad) for g in gus]
    gate_mine, gate_other = columns_grad(0, rows, gus, form)

    def scatter_z(v):
        v = lax.psum_scatter(v, "z", scatter_dimension=0, tiled=True)
        return lax.psum(v, "r") if n_r > 1 else v

    def pieces(v):
        v = v.reshape(2, n_s, -1, ff_pad)
        v = natural([pick(v, s, 1)] + [px(pick(v, s ^ k, 1), k) for k in range(1, n_s)], s)
        v = lax.all_gather(v.reshape(-1, ff_pad), "z", axis=0, tiled=True)
        return v.reshape(n_z, n_s, 2, -1, ff_pad)

    if n_r > 1:
        gw_down = lax.psum(gw_down, "r")
    gw_down = lax.all_gather(gw_down, "z", axis=0, tiled=True)
    gw_up = up_mine + pc(up_other)
    gw_gate = gate_mine + pc(gate_other)
    gw_gu = jnp.stack([gw_gate, gw_up], axis=1).reshape(-1, ff_pad)
    nffn_grad = after(nffn_grad, gw_gu)
    gw_gu = scatter_z(gw_gu)

    res_grad = zf + rms_back(residual, r_res, gf_in, nffn_grad)
    gg_ffn_in = jnp.sum(nffn_grad * residual * r_res, axis=0)
    gg_attn_out = jnp.sum(res_grad * attn_out * r_ao, axis=0)
    attn_grad = whole(rms_back(attn_out, r_ao, ga_out, res_grad).astype(BF))
    def to_shards(v):
        v = v.reshape(n_s, v.size // (n_s * v.shape[-1]), v.shape[-1])
        parts = [pick(v, s ^ k) for k in range(n_s)]
        return scatter4([parts[0].astype(F32)] + parts[1:]).astype(BF)

    gw_out = dot_rows(mixed, attn_grad).astype(BF).reshape(heads, 2, HD // 2, width)
    there = pc(pick(gw_out, 1 - c, 1))
    gw_out = to_shards(by_core(pick(gw_out, c, 1), there, 0))
    mixed_grad = dot_t(attn_grad, w_out_mine).astype(BF)
    q_low, k_grad, v_grad, gg_query = attend_back(
        at, queries, keys, values, mixed_grad, raw, gq, cos, sin
    )
    k_grad = k_grad + pc(k_grad.astype(BF)).astype(F32)
    v_grad = v_grad + pc(v_grad.astype(BF)).astype(F32)
    if n_r > 1:
        k_grad = lax.psum_scatter(k_grad.astype(BF), "r", scatter_dimension=0, tiled=True).astype(F32)
        v_grad = lax.psum_scatter(v_grad.astype(BF), "r", scatter_dimension=0, tiled=True).astype(F32)
    k_raw = raw[:, hw:]
    rk = inv_rms(k_raw)
    k_un = rope(k_grad, cos, -sin)
    gg_key = jnp.sum(rows_of(k_un * k_raw * rk, c), axis=0)
    k_low = rms_back(k_raw, rk, gk, k_un).astype(BF)
    v_low = v_grad.astype(BF)
    low_own = jnp.concatenate([rows_of(q_low, c), rows_of(k_low, c), rows_of(v_low, c)], axis=1)
    nin_grad = dot_t(low_own, w_qkv) + dot_t(pc(rows_of(q_low, 1 - c)), wq_other)
    gg_attn_in = jnp.sum(nin_grad * x * r_x, axis=0)
    input_grad = (res_grad + rms_back(x, r_x, ga_in, nin_grad)).astype(BF)

    low_mine = jnp.concatenate([q_low, jnp.where(c == 0, k_low, v_low)], axis=1)
    gw_qkv = dot_rows(nin, low_mine).astype(BF)
    cols = gw_qkv.shape[1]
    parts = [gg_attn_in, gg_attn_out, gg_ffn_in, gg_ffn_out, gg_query, gg_key]
    small = jnp.concatenate([p.reshape(n_s, -1) for p in parts], axis=1)
    count = small.shape[1]
    out_rows = gw_out.size // cols
    extra = -(-(d_own + out_rows + -(-count // cols)) // (16 * n_z)) * (16 * n_z) - d_own - out_rows
    small = jnp.pad(small, ((0, 0), (0, extra * cols - count))).reshape(n_s, extra, cols)
    gw_qkv = jnp.concatenate([gw_qkv.reshape(n_s, d_own, cols), small.astype(BF)], axis=1)
    parts = [pick(gw_qkv, s ^ k) for k in range(n_s)]
    parts[0] = parts[0].astype(F32)
    hop_a, hop_b = scatter_first(parts)
    sent = scatter_second(parts, hop_a, hop_b)
    gw_qkv = scatter_last(parts, sent).astype(BF)
    line = Line(jnp.concatenate([gw_qkv, gw_out.reshape(out_rows, cols)]))
    gw_gu = pieces(after(gw_gu, gw_qkv))
    line.middle(gw_qkv)
    line.last(gw_qkv)
    gw_attn = line.done(gw_qkv)
    input_grad = after(input_grad, gw_gu)
    input_grad = in_order(spread(input_grad.reshape(tokens.shape)))

    attn_there = pc(gw_attn)
    gw_qkv, qkv_there = gw_attn[: d_own + extra], attn_there[: d_own + extra]
    gw_out, out_there = (
        v[d_own + extra :].reshape(half_head, width) for v in (gw_attn, attn_there)
    )
    small = (gw_qkv[d_own:].astype(F32) + qkv_there[d_own:].astype(F32)).reshape(-1)
    small_out = []
    first = 0
    for size in [d_own] * 4 + [hd_own] * 2:
        small_out.append(small[first : first + size])
        first += size
    qkv_pair = by_core(gw_qkv[:d_own], qkv_there[:d_own], 0).astype(F32)
    gw_query = jnp.concatenate([qkv_pair[0][:, :hw], qkv_pair[1][:, :hw]], axis=1)
    gw_key, gw_value = qkv_pair[0][:, hw:], qkv_pair[1][:, hw:]
    gw_out = by_core(gw_out, out_there, 0).reshape(w_out.shape).astype(F32)
    gw_down = by_core(gw_down, pc(gw_down), 0).reshape(w_down.shape).astype(F32)
    gw_gate, gw_up = lay(at, gw_gu, pc(gw_gu), ff_own)
    return (
        output,
        input_grad,
        gw_query,
        gw_key,
        gw_value,
        gw_out,
        gw_gate,
        gw_up,
        gw_down,
        *small_out,
    )


def solution(mesh):
    n_s, n_c = mesh.shape["shard"], mesh.shape["ctx"]

    def run(*args):
        seqs = args[0].shape[0] // n_s
        groups = n_c // (2 * seqs)
        fine = Mesh(mesh.devices.reshape(n_s, groups, seqs, 2), ("shard", "r", "z", "c"))
        ctx = ("r", "z", "c")
        rows, mat, vec = P("shard", ctx, None), P("shard", None), P("shard")
        return jax.shard_map(
            body,
            mesh=fine,
            in_specs=(rows, rows, mat) + (mat,) * 7 + (vec,) * 6,
            out_specs=(rows, rows) + (mat,) * 7 + (vec,) * 6,
            check_vma=False,
        )(*args)

    return run
```
